128 devices in a mesh: blk: 32 (over x, y, core), mp: 4 (over z).
Axes of the slice: x: 4, y: 4, z: 4, core: 2. Of those that a mesh axis runs over, the one named last changes fastest.
Arguments:
- hidden: bfloat16 [144, 3584], replicated, may hold values from -6 to 6
- medusa_w: bfloat16 [2, 3584, 3584], P(None, 'blk', 'mp'), may hold values from -0.09375 to 0.09375
- embedding: bfloat16 [131072, 3584], P(('blk', 'mp')), may hold values from -0.5 to 0.5
- cand_ids: int32 [2, 144, 10], replicated, may hold values from 0 to 131071
- tree_q: bfloat16 [12, 48, 4096], P(None, None, 'mp'), may hold values from -6 to 6
- tree_key_value: bfloat16 [2, 12, 48, 2048], P(None, None, None, 'mp'), may hold values from -6 to 6
- prompt_key_value: bfloat16 [2, 32, 2048, 2048], P(None, 'blk', None, 'mp'), may hold values from -6 to 6
- block_group: int32 [32], P('blk'), may hold values from 0 to 11, as said below
- block_len: int32 [32], P('blk'), may hold values from 1 to 2048
- block_empty: int32 [32], P('blk'), may hold values 0 or 1
- parents: int32 [12, 48], replicated, may hold values from 0 to 46, as said below
- out_weight: bfloat16 [4096, 3584], P('mp'), may hold values from -0.09375 to 0.09375
- post_gain: float32 [3584], replicated, may hold values from 0.5 to 1.5
- resid: bfloat16 [576, 3584], P('blk'), may hold values from -6 to 6
Outputs:
- draft_logprob: float32 [2, 144, 10], replicated
- layer_out: bfloat16 [576, 3584], P('blk')
The draws below stay inside these ranges and needn't reach their ends.
Inputs may be any that keep to these rules, and one draw needn't show every extreme that they name: `block_group`: every group number from 0 to min(12, 32) - 1 owns at least one block. `parents`: entry 0 of each row is 0; entry i for i >= 1 is below i; some group's last token has parent 48 - 2.
All inputs are finite; a program needn't handle non-finite values. No bound on the sum of `block_empty` on one device may be relied on, other than what follows from the above.
Results may differ from the reference program's by a relative error of at most 0.005.
Values may be sent and summed in bfloat16 or wider, within the bound.
A program may use at most 128 MiB of HBM per device.

```python
import jax
import jax.numpy as jnp
from jax import lax

D = 3584
HQ = 16
KEY_VALUE_HEADS = 8
HEAD_SIZE = 256
VOC = 131072
MEDUSA = 2
TOPC = 10
ROWS = 144
PROMPT_GROUPS = 12
TREE_TOKENS = 48
BLOCK_SLOTS = 2048
PROMPT_BLOCKS = 32
TOKENS = 576


def draw_block_group(key, part):
    column = jnp.arange(PROMPT_BLOCKS, dtype=jnp.int32)
    random_groups = jax.random.randint(key, (PROMPT_BLOCKS,), 0, PROMPT_GROUPS, dtype=jnp.int32)
    groups = jnp.where(column < PROMPT_GROUPS, column, random_groups)
    return jax.random.permutation(jax.random.fold_in(key, 1), groups)


def draw_block_len(key, part):
    lengths = jax.random.randint(key, (PROMPT_BLOCKS,), 1, BLOCK_SLOTS + 1, dtype=jnp.int32)
    lengths = lengths.at[0].set(BLOCK_SLOTS).at[1].set(1)
    return jax.random.permutation(jax.random.fold_in(key, 1), lengths)


def draw_parents(key, part):
    column = jnp.arange(TREE_TOKENS, dtype=jnp.int32)
    upper = jnp.maximum(column, 1)
    picks = jax.random.randint(key, (PROMPT_GROUPS, TREE_TOKENS), 0, upper[None, :], dtype=jnp.int32)
    picks = jnp.where(column[None, :] == 0, 0, picks).astype(jnp.int32)
    return picks.at[0, TREE_TOKENS - 1].set(TREE_TOKENS - 2)


def plant(drawn, own_key, least, largest):
    extent = drawn.shape
    spot = [jax.random.randint(jax.random.fold_in(own_key, axis), (), 0, extent[axis]) for axis in range(len(extent))]
    drawn = drawn.at[tuple(spot)].set(least)
    longest = extent.index(max(extent))
    spot[longest] = (spot[longest] + 1) % extent[longest]
    return drawn.at[tuple(spot)].set(largest)


def levels(stream_key, shape, shards, least, high):
    def one(position, shards_of):
        draws = jax.random.uniform(jax.random.fold_in(jax.random.fold_in(stream_key, 6), position), (shards_of,), jnp.float32, least / len(shards), high / len(shards))
        return jnp.repeat(jnp.exp(draws), shape[position] // shards_of).reshape((-1,) + (1,) * (len(shape) - position - 1))

    level = one(*shards[0])
    for cut in shards[1:]:
        level = level * one(*cut)
    return level


def centred(own_key, extent, scale, most, shards=(), kind=jnp.bfloat16):
    factor_of = levels(own_key, extent, shards, -0.22, 0.18) if shards else 1.0
    entries = jax.random.normal(own_key, extent, jnp.float32) * scale * factor_of
    return jnp.minimum(jnp.maximum(entries, -most), most).astype(kind)


def setup_inputs(seed: int = 0) -> dict:
    key_of = jax.random.split(jax.random.key(seed), 15)
    return {
        "hidden": centred(key_of[0], (ROWS, D), 1.0, 6.0),
        "medusa_w": centred(key_of[1], (MEDUSA, D, D), D ** -0.5, 0.09375, ((1, 32), (2, 4))),
        "embedding": centred(key_of[2], (VOC, D), (D // 25) ** -0.5, 0.5, ((0, 128),)),
        "cand_ids": plant(jax.random.randint(key_of[3], (MEDUSA, ROWS, TOPC), 0, VOC), jax.random.fold_in(key_of[3], 1), 0, VOC - 1).astype(jnp.int32),
        "tree_q": centred(key_of[4], (PROMPT_GROUPS, TREE_TOKENS, HQ * HEAD_SIZE), 1.0, 6.0, ((2, 4),)),
        "tree_key_value": centred(key_of[5], (2, PROMPT_GROUPS, TREE_TOKENS, KEY_VALUE_HEADS * HEAD_SIZE), 1.0, 6.0, ((3, 4),)),
        "prompt_key_value": centred(key_of[6], (2, PROMPT_BLOCKS, BLOCK_SLOTS, KEY_VALUE_HEADS * HEAD_SIZE), 1.0, 6.0, ((1, 32), (3, 4))),
        "block_group": draw_block_group(jax.random.fold_in(key_of[14], 71), 0),
        "block_len": draw_block_len(jax.random.fold_in(key_of[14], 71), 0),
        "block_empty": plant((jax.random.randint(key_of[9], (PROMPT_BLOCKS,), 0, 4) < 1).astype(jnp.int32), jax.random.fold_in(key_of[9], 1), 0, 1),
        "parents": draw_parents(jax.random.fold_in(key_of[14], 71), 0),
        "out_weight": centred(key_of[11], (HQ * HEAD_SIZE, D), (HQ * HEAD_SIZE) ** -0.5, 0.09375, ((0, 4),)),
        "post_gain": jnp.clip(1.0 + 0.1 * jax.random.normal(key_of[12], (D,), jnp.float32), 0.5, 1.5),
        "resid": centred(key_of[13], (TOKENS, D), 1.0, 6.0, ((0, 32),)),
    }


def capped(values, limit):
    return limit * jnp.tanh(values / limit)

def ancestry(parents):
    count = parents.shape[1]
    column = jnp.arange(count, dtype=jnp.int32)
    linked = (parents[:, :, None] == column[None, None, :]) & (column[None, :, None] > 0)
    reach = jnp.eye(count, dtype=jnp.float32)[None] + linked.astype(jnp.float32)
    for sweep in range(count.bit_length()):
        reach = jnp.minimum(jnp.einsum('gij,gjk->gik', reach, reach, precision=lax.Precision.HIGHEST), 1.0)
    return reach

def attend(queries, keys, values, mask):
    rows = queries.shape[0]
    length = keys.shape[0]
    kv_heads = keys.shape[1] // HEAD_SIZE
    repeats = queries.shape[1] // keys.shape[1]
    query_view = queries.astype(jnp.float32).reshape(rows, kv_heads, repeats, HEAD_SIZE)
    key_view = keys.astype(jnp.float32).reshape(length, kv_heads, HEAD_SIZE)
    value_view = values.astype(jnp.float32).reshape(length, kv_heads, HEAD_SIZE)
    scores = jnp.einsum('qhrd,khd->hrqk', query_view, key_view) * HEAD_SIZE ** (-0.5)
    weights = jnp.exp(capped(scores, 50.0)) * mask[None, None]
    denominator = lax.optimization_barrier(jnp.sum(weights, -1)).transpose(2, 0, 1).reshape(rows, kv_heads * repeats)
    rounded = lax.optimization_barrier(weights.astype(jnp.bfloat16)).astype(jnp.float32)
    numerator = jnp.einsum('hrqk,khd->qhrd', rounded, value_view).reshape(rows, kv_heads * repeats * HEAD_SIZE)
    return (numerator, denominator)

def reference(hidden, medusa_w, embedding, cand_ids, tree_q, tree_key_value, prompt_key_value, block_group, block_len, block_empty, parents, out_weight, post_gain, resid):
    results = []
    for head in range(MEDUSA):
        inner = jnp.dot(hidden, medusa_w[head], preferred_element_type=jnp.float32)
        fresh = (hidden.astype(jnp.float32) + jax.nn.silu(inner)).astype(jnp.bfloat16)
        logits = capped(jnp.dot(fresh, embedding.T, preferred_element_type=jnp.float32), 30.0)
        total = lax.optimization_barrier(jnp.sum(jnp.exp(logits), -1))
        picked = jnp.take_along_axis(logits, cand_ids[head], axis=1)
        results.append(picked - jnp.log(total)[:, None])
    draft_logprob = jnp.stack(results)
    positions = jnp.arange(BLOCK_SLOTS, dtype=jnp.int32)
    numer_init = jnp.zeros((PROMPT_GROUPS, TREE_TOKENS, HQ * HEAD_SIZE), jnp.float32)
    denom_init = jnp.zeros((PROMPT_GROUPS, TREE_TOKENS, HQ), jnp.float32)

    def visit(carry, item):
        numer, denom = carry
        keys, values, group, length, empty = item
        queries = lax.dynamic_index_in_dim(tree_q, group, 0, keepdims=False)
        key_ok = ((positions < length) & (empty == 0)).astype(jnp.float32)
        mask = jnp.broadcast_to(key_ok[None, :], (TREE_TOKENS, BLOCK_SLOTS))
        more_numer, more_denom = attend(queries, keys, values, mask)
        numer = lax.dynamic_update_index_in_dim(numer, lax.dynamic_index_in_dim(numer, group, 0, keepdims=False) + more_numer, group, 0)
        denom = lax.dynamic_update_index_in_dim(denom, lax.dynamic_index_in_dim(denom, group, 0, keepdims=False) + more_denom, group, 0)
        return ((numer, denom), None)
    scanned = lax.scan(visit, (numer_init, denom_init), (prompt_key_value[0], prompt_key_value[1], block_group, block_len, block_empty))
    numer, denom = scanned[0]
    reach = ancestry(parents)
    tree_numer, tree_denom = jax.vmap(attend)(tree_q, tree_key_value[0], tree_key_value[1], reach)
    numer = numer + tree_numer
    denom = denom + tree_denom
    heads_out = (numer.reshape(PROMPT_GROUPS, TREE_TOKENS, HQ, HEAD_SIZE) / denom[..., None]).reshape(TOKENS, HQ * HEAD_SIZE).astype(jnp.bfloat16)
    attn = jnp.dot(heads_out, out_weight, preferred_element_type=jnp.float32)
    normed = attn * lax.rsqrt(lax.optimization_barrier(jnp.mean(attn * attn, -1, keepdims=True)) + 1e-06) * post_gain
    layer_out = (normed + resid.astype(jnp.float32)).astype(jnp.bfloat16)
    return (draft_logprob, layer_out)
```

```python
import jax
import jax.numpy as jnp
from jax import lax
from jax.experimental import pallas as pl
from jax.experimental.pallas import tpu as pltpu
from jax.sharding import PartitionSpec as P

MESH = pl.DeviceIdType.MESH
F32 = jnp.float32
BF16 = jnp.bfloat16

D = 3584
ROWS = 144
MROWS = 288
UNITS = 896
DEPTH = 112
GROUPS = 12
TREE = 48
HEAD = 256
HEADS = 4
SLOTS = 2048
VOCAB = 1024
TOPC = 10
NB = 32
OWNERS = (0, 11, 22)
KEY_TILE = 512
NT = (((1,), (1,)), ((), ()))
NN = (((1,), (0,)), ((), ()))


def dot(a, b, dims=NN):
    return lax.dot_general(a, b, dims, preferred_element_type=F32)


def iota(shape, axis):
    return lax.broadcasted_iota(jnp.int32, shape, axis)


def weigh(scores):
    return jnp.exp(50.0 * jnp.tanh(scores * (HEAD ** (-0.5) / 50.0)))


SCRATCH = (
    ("hwin", pltpu.VMEM((ROWS, 256), BF16)),
    ("wpad", pltpu.VMEM((2, 256, UNITS), BF16)),
    ("hown", pltpu.VMEM((2, 32, 128), BF16)),
    ("embv", pltpu.VMEM((VOCAB, D), BF16)),
    ("outv", pltpu.VMEM((HEADS * HEAD, D), BF16)),
    ("kbuf", pltpu.VMEM((SLOTS, 512), BF16)),
    ("vbuf", pltpu.VMEM((SLOTS, 512), BF16)),
    ("qbuf", pltpu.VMEM((GROUPS, TREE, 1024), BF16)),
    ("tqb", pltpu.VMEM((GROUPS, 64, HEAD), BF16)),
    ("tkb", pltpu.VMEM((GROUPS, 64, HEAD), BF16)),
    ("tvb", pltpu.VMEM((GROUPS, 64, HEAD), BF16)),
    ("candv", pltpu.VMEM((2, ROWS, TOPC), jnp.int32)),
    ("parv", pltpu.VMEM((GROUPS, TREE), jnp.int32)),
    ("gainv", pltpu.VMEM((1, D), F32)),
    ("residv", pltpu.VMEM((18, D), BF16)),
    ("sem_in", pltpu.SemaphoreType.DMA((20,))),
    ("pbuf", pltpu.VMEM((64, 32, 128), BF16)),
    ("precv", pltpu.VMEM((NB - 1, 2, 32, 128), BF16)),
    ("ps", pltpu.SemaphoreType.DMA),
    ("pr", pltpu.SemaphoreType.DMA),
    ("f0", pltpu.VMEM((4, 2, 4, 4, 32, 128), BF16)),
    ("f1", pltpu.VMEM((4, 2, 4, 4, 32, 128), BF16)),
    ("fz_s", pltpu.SemaphoreType.DMA((2,))),
    ("fz_r", pltpu.SemaphoreType.DMA((2,))),
    ("fa_s", pltpu.SemaphoreType.DMA((2,))),
    ("fa_r", pltpu.SemaphoreType.DMA((2,))),
    ("fb_s", pltpu.SemaphoreType.DMA((2,))),
    ("fb_r", pltpu.SemaphoreType.DMA((2, 3))),
    ("fc_s", pltpu.SemaphoreType.DMA((2,))),
    ("fc_r", pltpu.SemaphoreType.DMA((2,))),
    ("fresh", pltpu.VMEM((MROWS, D), BF16)),
    ("abuf", pltpu.VMEM((NB, 8, 384), BF16)),
    ("arecv", pltpu.VMEM((NB, 8, 384), BF16)),
    ("as_", pltpu.SemaphoreType.DMA),
    ("ar", pltpu.SemaphoreType.DMA),
    ("treen", pltpu.VMEM((GROUPS, 8, HEAD), F32)),
    ("treed", pltpu.VMEM((GROUPS, 8, 128), F32)),
    ("hbuf", pltpu.VMEM((GROUPS, 8, HEAD), BF16)),
    ("hrecv", pltpu.VMEM((GROUPS, 8, HEAD), BF16)),
    ("hs", pltpu.SemaphoreType.DMA((GROUPS,))),
    ("hr", pltpu.SemaphoreType.DMA),
    ("zbuf", pltpu.VMEM((4, 3, 8, D), BF16)),
    ("zs", pltpu.SemaphoreType.DMA),
    ("zr", pltpu.SemaphoreType.DMA),
    ("nrm", pltpu.VMEM((24, D), F32)),
    ("idv", pltpu.VMEM((384, 128), F32)),
    ("sbuf", pltpu.VMEM((4, 16, 384), F32)),
    ("ss", pltpu.SemaphoreType.DMA),
    ("sr", pltpu.SemaphoreType.DMA),
    ("sown", pltpu.VMEM((3, 16, 128), F32)),
    ("grecv", pltpu.VMEM((NB, 16, 128), F32)),
    ("gs", pltpu.SemaphoreType.DMA((3,))),
    ("gr", pltpu.SemaphoreType.DMA),
    ("rbuf", pltpu.VMEM((3, 16, 128), F32)),
    ("rs", pltpu.SemaphoreType.DMA),
    ("rr", pltpu.SemaphoreType.DMA((3,))),
)


class Refs:
    pass


def kernel(
    hidden, medusa_w, embedding, cand_ids, tree_q, tree_kv, prompt_kv,
    block_group, block_len, block_empty, parents, out_weight, post_gain, resid,
    out_ref, stat_ref, *scratch
):
    s = Refs()
    for (name, _), ref in zip(SCRATCH, scratch):
        setattr(s, name, ref)
    me = lax.axis_index("blk")
    mz = lax.axis_index("mp")
    mx, my, mc = me // 8, (me // 2) % 4, me % 2
    head, part = me // 8, me % 8

    def peer_of(step):
        return lax.rem(me + step, NB)

    def z_of(step):
        return lax.rem(mz + step, 4)

    def remote(src, dst, ss, rs, **where):
        return pltpu.make_async_remote_copy(
            src_ref=src, dst_ref=dst, send_sem=ss, recv_sem=rs,
            device_id=where, device_id_type=MESH,
        )

    def drain(ref, sem):
        pltpu.make_async_copy(ref, ref, sem).wait()

    inputs = []

    def fetch(src, dst):
        copy = pltpu.make_async_copy(src, dst, s.sem_in.at[len(inputs)])
        copy.start()
        inputs.append(copy)
        return copy

    first = DEPTH * me
    start = jnp.minimum((first // 128) * 128, D - 256)
    start = pl.multiple_of(start, 128)
    shift = pl.multiple_of(first - start, 16)
    for m in range(2):
        s.wpad[m] = jnp.zeros((256, UNITS), BF16)
    in_w = [
        fetch(hidden.at[:, pl.ds(start, 256)], s.hwin),
        fetch(medusa_w.at[0], s.wpad.at[0, pl.ds(shift, DEPTH), :]),
        fetch(medusa_w.at[1], s.wpad.at[1, pl.ds(shift, DEPTH), :]),
    ]
    in_q = fetch(tree_q, s.qbuf)
    in_k = fetch(prompt_kv.at[0, 0], s.kbuf)
    in_v = fetch(prompt_kv.at[1, 0], s.vbuf)
    in_h = []
    for p in range(2):
        chunk = 2 * me + p
        rblk, lane = chunk // 7, chunk % 7
        col = pl.multiple_of(mz * UNITS + lane * 128, 128)
        for half in range(2):
            row = pl.multiple_of(((rblk * 2 + half) % 9) * 16, 16)
            in_h.append(
                fetch(
                    hidden.at[pl.ds(row, 16), pl.ds(col, 128)],
                    s.hown.at[p, pl.ds(half * 16, 16), :],
                )
            )
    qcol = pl.multiple_of(head * HEAD, HEAD)
    kcol = pl.multiple_of((head // 2) * HEAD, HEAD)
    in_t = [
        fetch(tree_q.at[:, :, pl.ds(qcol, HEAD)], s.tqb.at[:, pl.ds(0, TREE), :]),
        fetch(tree_kv.at[0, :, :, pl.ds(kcol, HEAD)], s.tkb.at[:, pl.ds(0, TREE), :]),
        fetch(tree_kv.at[1, :, :, pl.ds(kcol, HEAD)], s.tvb.at[:, pl.ds(0, TREE), :]),
        fetch(parents, s.parv),
    ]
    in_c = fetch(cand_ids, s.candv)
    in_o = fetch(out_weight, s.outv)
    in_g = [fetch(post_gain, s.gainv), fetch(resid, s.residv)]
    in_e = fetch(embedding, s.embv)

    barrier = pltpu.get_barrier_semaphore()

    def greet(step, carry):
        pl.semaphore_signal(
            barrier, inc=1, device_id={"blk": peer_of(step)}, device_id_type=MESH
        )
        return carry

    lax.fori_loop(1, NB, greet, 0)
    for step in range(1, 4):
        pl.semaphore_signal(
            barrier, inc=1, device_id={"mp": z_of(step)}, device_id_type=MESH
        )

    for copy in in_w:
        copy.wait()
    hwin = s.hwin[...]
    for m in range(2):
        product = dot(hwin, s.wpad[m]).astype(BF16)
        for u in range(9):
            unit = m * 9 + u
            for lane in range(7):
                s.pbuf[(unit // 2) * 7 + lane, (unit % 2) * 16:(unit % 2) * 16 + 16, :] = (
                    product[u * 16:u * 16 + 16, lane * 128:lane * 128 + 128]
                )
    s.pbuf[63] = jnp.zeros((32, 128), BF16)
    pl.semaphore_wait(barrier, NB - 1 + 3)

    def send_product(step, carry):
        peer = peer_of(step)
        remote(
            s.pbuf.at[pl.ds(2 * peer, 2)], s.precv.at[step - 1], s.ps, s.pr, blk=peer
        ).start()
        return carry

    lax.fori_loop(1, NB, send_product, 0)

    group = block_group[0]
    limit = jnp.where(block_empty[0] == 0, block_len[0], 0)
    spread = (
        (iota((64, TREE), 0) // 8) * 6 + iota((64, TREE), 0) % 8 == iota((64, TREE), 1)
    ) & (iota((64, TREE), 0) % 8 < 6)
    spread = spread.astype(F32).astype(BF16)
    in_q.wait()
    queries = dot(spread, s.qbuf[group]).astype(BF16)
    in_k.wait()
    in_v.wait()
    row8 = iota((8, 384), 0)
    lane8 = iota((8, 384), 1)
    tag = jnp.full((8, 384), group, jnp.int32).astype(F32)
    for kv in range(2):
        cols = slice(kv * HEAD, kv * HEAD + HEAD)
        two = jnp.concatenate(
            [queries[:, (2 * kv + r) * HEAD:(2 * kv + r + 1) * HEAD] for r in range(2)], 0
        )
        numer = jnp.zeros((128, HEAD), F32)
        denom = jnp.zeros((128, 128), F32)
        for tile in range(SLOTS // KEY_TILE):
            keys = slice(tile * KEY_TILE, tile * KEY_TILE + KEY_TILE)
            seen = iota((128, KEY_TILE), 1) + tile * KEY_TILE < limit
            weight = jnp.where(seen, weigh(dot(two, s.kbuf[keys, cols], NT)), 0.0)
            for piece in range(KEY_TILE // 128):
                denom = denom + weight[:, piece * 128:piece * 128 + 128]
            numer = numer + dot(weight.astype(BF16), s.vbuf[keys, cols])
        total = jnp.broadcast_to(jnp.sum(denom, 1, keepdims=True), (128, 128))
        high = total.astype(BF16).astype(F32)
        pair = jnp.where(iota((128, 128), 1) < 64, high, total - high)
        both = jnp.concatenate([numer, pair], 1)
        for r in range(2):
            for q in range(8):
                rows = both[r * 64 + q * 8:r * 64 + q * 8 + 8]
                s.abuf[(2 * kv + r) * 8 + q] = jnp.where(row8 < 6, rows, tag).astype(BF16)

    def send_attention(step, carry):
        peer = peer_of(step)
        remote(s.abuf.at[peer], s.arecv.at[step], s.as_, s.ar, blk=peer).start()
        return carry

    lax.fori_loop(1, NB, send_attention, 0)
    s.arecv[0] = s.abuf[me]

    for copy in in_h:
        copy.wait()
    drain(s.precv, s.pr)
    inner = lax.fori_loop(
        0, NB - 1,
        lambda i, acc: acc + s.precv[i].astype(F32),
        s.pbuf[pl.ds(2 * me, 2)].astype(F32),
    )
    fresh = (s.hown[...].astype(F32) + inner / (1.0 + jnp.exp(-inner))).astype(BF16)
    s.f0[my, mc, mx, mz] = fresh[0]
    s.f1[mx, mc, my, mz] = fresh[1]
    for step in range(1, 4):
        for which, own in enumerate((s.f0.at[my, mc, mx, mz], s.f1.at[mx, mc, my, mz])):
            remote(own, own, s.fz_s.at[which], s.fz_r.at[which], mp=z_of(step)).start()

    for copy in in_t:
        copy.wait()
    for buf in (s.tqb, s.tkb, s.tvb):
        for g in range(GROUPS):
            buf[g, TREE:64, :] = jnp.zeros((64 - TREE, HEAD), BF16)
    place = (iota((TREE, 256), 0) == iota((TREE, 256), 1) % 64).astype(F32).astype(BF16)
    spots = dot(s.parv[...].astype(F32).astype(BF16), place)
    sub = iota((256, 256), 0)
    lan = iota((256, 256), 1)
    eye = sub == lan
    pick_row = iota((32, 256), 0)
    pick_col = iota((32, 256), 1)
    pick = (pick_col == (pick_row // 8) * 64 + part * 6 + pick_row % 8) & (pick_row % 8 < 6)
    pick = pick.astype(F32).astype(BF16)
    for b in range(3):
        mine = iota((GROUPS, 256), 0) == 4 * b + iota((GROUPS, 256), 1) // 64
        parent = jnp.sum(jnp.where(mine, spots, 0.0), 0, keepdims=True)
        wanted = parent + (iota((1, 256), 1) // 64 * 64).astype(F32)
        linked = (sub.astype(F32) == wanted) & (lan % 64 > 0)
        reach = jnp.where(eye | linked, 1.0, 0.0).astype(BF16)
        for sweep in range(6):
            reach = jnp.minimum(dot(reach, reach), 1.0).astype(BF16)
        mask = dot(pick, reach, NT)
        tq = s.tqb[4 * b:4 * b + 4].reshape(256, HEAD)
        tk = s.tkb[4 * b:4 * b + 4].reshape(256, HEAD)
        tv = s.tvb[4 * b:4 * b + 4].reshape(256, HEAD)
        rows = dot(pick, tq).astype(BF16)
        weight = weigh(dot(rows, tk, NT)) * mask
        numer = dot(weight.astype(BF16), tv)
        denom = jnp.broadcast_to(jnp.sum(weight, 1, keepdims=True), (32, 128))
        s.treen[4 * b:4 * b + 4] = numer.reshape(4, 8, HEAD)
        s.treed[4 * b:4 * b + 4] = denom.reshape(4, 8, 128)

    def x_peer(step):
        return lax.rem(mx + step, 4) * 8 + my * 2 + mc

    def y_peer(step):
        return mx * 8 + lax.rem(my + step, 4) * 2 + mc

    lines = ((s.f0, my, mx, x_peer, y_peer), (s.f1, mx, my, y_peer, x_peer))
    for which, (buf, slow, quick, near, far) in enumerate(lines):
        drain(buf.at[slow, mc, quick, pl.ds(0, 3)], s.fz_r.at[which])
        own = buf.at[slow, mc, quick]
        for step in range(1, 4):
            remote(own, own, s.fa_s.at[which], s.fa_r.at[which], blk=near(step)).start()

    drain(s.arecv.at[pl.ds(1, NB - 1)], s.ar)
    for half in range(2):
        def add(i, carry):
            got = s.arecv[i].astype(F32)
            named = jnp.broadcast_to(got[6:7], (8, 384))
            return tuple(
                acc + jnp.where(named == float(half * 6 + g), got, 0.0)
                for g, acc in enumerate(carry)
            )

        sums = lax.fori_loop(0, NB, add, (jnp.zeros((8, 384), F32),) * 6)
        for g in range(6):
            both = sums[g]
            pair = both[:, HEAD:]
            denom = pair[:, :1] + pair[:, 64:65] + s.treed[half * 6 + g][:, :1]
            denom = jnp.where(iota((8, 1), 0) < 6, denom, 1.0)
            numer = both[:, :HEAD] + s.treen[half * 6 + g]
            numer = jnp.where(iota((8, HEAD), 0) < 6, numer, 0.0)
            s.hbuf[half * 6 + g] = (numer / denom).astype(BF16)

    def heads_copy(g):
        chunk = g * 8 + part
        owner = chunk // 3
        spot = (chunk % 3) * 4 + head
        return owner, spot

    def send_heads(g, carry):
        owner, spot = heads_copy(g)

        @pl.when(owner != me)
        def _():
            remote(
                s.hbuf.at[g], s.hrecv.at[spot], s.hs.at[g], s.hr, blk=owner
            ).start()

        @pl.when(owner == me)
        def _():
            pltpu.make_async_copy(s.hbuf.at[g], s.hrecv.at[spot], s.hr).start()

        return carry

    lax.fori_loop(0, GROUPS, send_heads, 0)

    sibling = me + 1 - 2 * mc
    for which, (buf, slow, quick, near, far) in enumerate(lines):
        drain(buf.at[slow, mc, pl.ds(0, 3)], s.fa_r.at[which])
        own = buf.at[slow, mc]
        for step in range(1, 4):
            remote(own, own, s.fb_s.at[which], s.fb_r.at[which, step - 1], blk=far(step)).start()
        remote(own, own, s.fc_s.at[which], s.fc_r.at[which], blk=sibling).start()

    in_o.wait()
    drain(s.hrecv, s.hr)
    lhs = jnp.concatenate(
        [
            jnp.concatenate([s.hrecv[t * 4 + h].astype(F32) for h in range(HEADS)], 1)
            for t in range(3)
        ],
        0,
    ).astype(BF16)
    for tile in range(7):
        cols = slice(tile * 512, tile * 512 + 512)
        got = dot(lhs, s.outv[:, cols]).astype(BF16)
        s.zbuf[mz, :, :, cols] = got.reshape(3, 8, 512)
    for step in range(1, 4):
        own = s.zbuf.at[mz]
        remote(own, own, s.zs, s.zr, mp=z_of(step)).start()

    in_c.wait()
    s.idv[...] = jnp.zeros((384, 128), F32)
    for m in range(2):
        s.idv[m * ROWS:m * ROWS + ROWS, 0:TOPC] = s.candv[m].astype(F32)
    ids = s.idv[...].T
    base = ((me * 4 + mz) * VOCAB).astype(F32)

    for step in range(1, 4):
        for which, (buf, slow, quick, near, far) in enumerate(lines):
            came = buf.at[lax.rem(slow - step + 4, 4), mc]
            drain(came, s.fb_r.at[which, step - 1])
            remote(came, came, s.fc_s.at[which], s.fc_r.at[which], blk=sibling).start()
    for which, (buf, slow, quick, near, far) in enumerate(lines):
        drain(buf.at[pl.ds(0, 2)], s.fc_r.at[which])

    def arrange(owner, carry):
        x, y, c = owner // 8, (owner // 2) % 4, owner % 2
        for p in range(2):
            chunk = 2 * owner + p
            row = pl.multiple_of((chunk // 7) * 32, 32)

            @pl.when(chunk < 63)
            def _():
                for z in range(4):
                    col = pl.multiple_of(z * UNITS + (chunk % 7) * 128, 128)
                    piece = s.f0[y, c, x, z] if p == 0 else s.f1[x, c, y, z]
                    s.fresh[pl.ds(row, 32), pl.ds(col, 128)] = piece

        return carry

    lax.fori_loop(0, NB, arrange, 0)

    in_e.wait()
    tall = iota((16, MROWS), 0)

    def score(tile, acc):
        rows = pl.multiple_of(tile * 256, 256)
        raw = dot(s.embv[pl.ds(rows, 256), :], s.fresh[...], NT)
        logits = 30.0 * jnp.tanh(raw * (1.0 / 30.0))
        acc = acc + jnp.where(tall == 0, jnp.sum(jnp.exp(logits), 0, keepdims=True), 0.0)
        here = (iota((256, MROWS), 0) + tile * 256).astype(F32) + base
        for c in range(TOPC):
            chosen = jnp.where(here == ids[c:c + 1, :MROWS], logits, 0.0)
            acc = acc + jnp.where(tall == c + 1, jnp.sum(chosen, 0, keepdims=True), 0.0)
        return acc

    stats = lax.fori_loop(0, 4, score, jnp.zeros((16, MROWS), F32))
    s.sbuf[mz] = jnp.concatenate([stats, jnp.zeros((16, 384 - MROWS), F32)], 1)
    for step in range(1, 4):
        own = s.sbuf.at[mz]
        remote(own, own, s.ss, s.sr, mp=z_of(step)).start()

    for copy in in_g:
        copy.wait()
    drain(s.zbuf.at[pl.ds(0, 3)], s.zr)
    attn = s.zbuf[0].astype(F32)
    for z in range(1, 4):
        attn = attn + s.zbuf[z].astype(F32)
    mean = jnp.sum(attn * attn, -1, keepdims=True) * (1.0 / D)
    normed = attn * lax.rsqrt(mean + 1e-06) * s.gainv[...][None]
    for t in range(3):
        s.nrm[6 * t:6 * t + 6, :] = normed[t, :6]
    out_ref[...] = (s.nrm[0:18, :] + s.residv[...].astype(F32)).astype(BF16)

    drain(s.sbuf.at[pl.ds(0, 3)], s.sr)
    summed = s.sbuf[0] + s.sbuf[1] + s.sbuf[2] + s.sbuf[3]
    for t in range(3):
        s.sown[t] = summed[:, t * 128:t * 128 + 128]
    for t in range(3):
        @pl.when(me != OWNERS[t])
        def _():
            remote(
                s.sown.at[t], s.grecv.at[me], s.gs.at[t], s.gr, blk=OWNERS[t]
            ).start()

    for t in range(3):
        @pl.when(me == OWNERS[t])
        def _():
            s.grecv[OWNERS[t]] = s.sown[t]
            drain(s.grecv.at[pl.ds(0, NB - 1)], s.gr)
            full = lax.fori_loop(
                1, NB, lambda i, acc: acc + s.grecv[i], s.grecv[0]
            )
            s.rbuf[t] = full - jnp.log(full[0:1])

            def tell(step, carry):
                remote(
                    s.rbuf.at[t], s.rbuf.at[t], s.rs, s.rr.at[t], blk=peer_of(step)
                ).start()
                return carry

            lax.fori_loop(1, NB, tell, 0)
            drain(s.grecv.at[pl.ds(0, NB - 1)], s.rs)

    for t in range(3):
        @pl.when(me != OWNERS[t])
        def _():
            drain(s.rbuf.at[t], s.rr.at[t])
            drain(s.sown.at[t], s.gs.at[t])

    stat_ref[...] = s.rbuf[...]

    drain(s.precv, s.ps)
    drain(s.arecv.at[pl.ds(1, NB - 1)], s.as_)
    for which, (buf, slow, quick, near, far) in enumerate(lines):
        drain(buf.at[slow, mc, quick, pl.ds(0, 3)], s.fz_s.at[which])
        drain(buf.at[slow, mc, pl.ds(0, 3)], s.fa_s.at[which])
        drain(buf.at[pl.ds(0, 3), mc], s.fb_s.at[which])
        drain(buf.at[pl.ds(0, 2)], s.fc_s.at[which])

    def sent_heads(g, carry):
        owner, spot = heads_copy(g)

        @pl.when(owner != me)
        def _():
            drain(s.hbuf.at[g], s.hs.at[g])

        return carry

    lax.fori_loop(0, GROUPS, sent_heads, 0)
    drain(s.zbuf.at[pl.ds(0, 3)], s.zs)
    drain(s.sbuf.at[pl.ds(0, 3)], s.ss)


def per_device(
    hidden, medusa_w, embedding, cand_ids, tree_q, tree_key_value, prompt_key_value,
    block_group, block_len, block_empty, parents, out_weight, post_gain, resid,
):
    anywhere = pl.BlockSpec(memory_space=pl.ANY)
    scalar = pl.BlockSpec(memory_space=pltpu.SMEM)
    whole = pl.BlockSpec(memory_space=pltpu.VMEM)
    layer_out, stats = pl.pallas_call(
        kernel,
        out_shape=(
            jax.ShapeDtypeStruct((18, D), BF16),
            jax.ShapeDtypeStruct((3, 16, 128), F32),
        ),
        in_specs=[anywhere] * 7 + [scalar] * 3 + [anywhere] * 4,
        out_specs=(whole, whole),
        scratch_shapes=[kind for _, kind in SCRATCH],
        compiler_params=pltpu.CompilerParams(
            collective_id=0, has_side_effects=True, vmem_limit_bytes=60 << 20
        ),
    )(
        hidden, medusa_w, embedding, cand_ids, tree_q, tree_key_value, prompt_key_value,
        block_group, block_len, block_empty, parents, out_weight,
        post_gain.reshape(1, D), resid,
    )
    picked = jnp.concatenate([stats[t, 1:1 + TOPC] for t in range(3)], 1)[:, :MROWS]
    return (picked.T.reshape(2, ROWS, TOPC), layer_out)


def solution(mesh):
    placed = (
        P(),
        P(None, "blk", "mp"),
        P(("blk", "mp"), None),
        P(),
        P(None, None, "mp"),
        P(None, None, None, "mp"),
        P(None, "blk", None, "mp"),
        P("blk"),
        P("blk"),
        P("blk"),
        P(),
        P("mp", None),
        P(),
        P("blk", None),
    )
    return jax.shard_map(
        per_device, mesh=mesh, in_specs=placed, out_specs=(P(), P("blk", None)), check_vma=False
    )
```

```python
import jax
import jax.numpy as jnp
from jax import lax
from jax.experimental import pallas as pl
from jax.experimental.pallas import tpu as pltpu
from jax.sharding import PartitionSpec as P

MESH = pl.DeviceIdType.MESH
F32 = jnp.float32
BF16 = jnp.bfloat16

D = 3584
ROWS = 144
MROWS = 288
UNITS = 896
DEPTH = 112
GROUPS = 12
TREE = 48
HEAD = 256
HEADS = 4
SLOTS = 2048
VOCAB = 1024
TOPC = 10
NB = 32
CHIPS = 16
KEY_TILE = 512
NT = (((1,), (1,)), ((), ()))
NN = (((1,), (0,)), ((), ()))


def dot(a, b, dims=NN):
    return lax.dot_general(a, b, dims, preferred_element_type=F32)


def iota(shape, axis):
    return lax.broadcasted_iota(jnp.int32, shape, axis)


def weigh(scores):
    return jnp.exp(50.0 * jnp.tanh(scores * (HEAD ** (-0.5) / 50.0)))


SCRATCH = (
    ("hwin", pltpu.VMEM((ROWS, 256), BF16)),
    ("wpad", pltpu.VMEM((2, 256, UNITS), BF16)),
    ("hown", pltpu.VMEM((2, 32, 128), BF16)),
    ("embv", pltpu.VMEM((VOCAB, D), BF16)),
    ("outv", pltpu.VMEM((HEADS * HEAD, D), BF16)),
    ("kbuf", pltpu.VMEM((SLOTS, 512), BF16)),
    ("vbuf", pltpu.VMEM((SLOTS, 512), BF16)),
    ("qbuf", pltpu.VMEM((GROUPS, TREE, 1024), BF16)),
    ("tqb", pltpu.VMEM((GROUPS, 64, HEAD), BF16)),
    ("tkb", pltpu.VMEM((GROUPS, 64, HEAD), BF16)),
    ("tvb", pltpu.VMEM((GROUPS, 64, HEAD), BF16)),
    ("candv", pltpu.VMEM((TOPC, 2, ROWS), jnp.int32)),
    ("parv", pltpu.VMEM((GROUPS, TREE), jnp.int32)),
    ("gainv", pltpu.VMEM((D,), F32)),
    ("residv", pltpu.VMEM((18, D), BF16)),
    ("sem_in", pltpu.SemaphoreType.DMA((20,))),
    ("pbuf", pltpu.VMEM((CHIPS, 2, 2, 32, 128), BF16)),
    ("psib", pltpu.VMEM((CHIPS, 2, 32, 128), BF16)),
    ("psum", pltpu.VMEM((CHIPS, 2, 32, 128), BF16)),
    ("precv", pltpu.VMEM((CHIPS - 1, 2, 32, 128), BF16)),
    ("pc_s", pltpu.SemaphoreType.DMA),
    ("pc_r", pltpu.SemaphoreType.DMA),
    ("ps", pltpu.SemaphoreType.DMA),
    ("pr", pltpu.SemaphoreType.DMA),
    ("f0", pltpu.VMEM((4, 2, 4, 4, 32, 128), BF16)),
    ("f1", pltpu.VMEM((4, 2, 4, 4, 32, 128), BF16)),
    ("fz_s", pltpu.SemaphoreType.DMA((2,))),
    ("fz_r", pltpu.SemaphoreType.DMA((2,))),
    ("fa_s", pltpu.SemaphoreType.DMA((2,))),
    ("fa_r", pltpu.SemaphoreType.DMA((2, 3))),
    ("fb_s", pltpu.SemaphoreType.DMA((2,))),
    ("fb_r", pltpu.SemaphoreType.DMA((2, 3))),
    ("fc_s", pltpu.SemaphoreType.DMA((2,))),
    ("fc_r", pltpu.SemaphoreType.DMA((2,))),
    ("fresh", pltpu.VMEM((MROWS, D), BF16)),
    ("abuf", pltpu.VMEM((NB, 8, HEAD), BF16)),
    ("arecv", pltpu.VMEM((NB, 8, HEAD), BF16)),
    ("as_", pltpu.SemaphoreType.DMA),
    ("ar", pltpu.SemaphoreType.DMA),
    ("treen", pltpu.VMEM((GROUPS, 8, HEAD), F32)),
    ("treed", pltpu.VMEM((GROUPS, 8, 128), F32)),
    ("hbuf", pltpu.VMEM((GROUPS, 8, HEAD), BF16)),
    ("hrecv", pltpu.VMEM((GROUPS, 8, HEAD), BF16)),
    ("hs", pltpu.SemaphoreType.DMA((GROUPS,))),
    ("hr", pltpu.SemaphoreType.DMA),
    ("zbuf", pltpu.VMEM((4, 3, 8, D), BF16)),
    ("zs", pltpu.SemaphoreType.DMA),
    ("zr", pltpu.SemaphoreType.DMA),
    ("nrm", pltpu.VMEM((24, D), F32)),
    ("idv", pltpu.VMEM((2, 16, 384), F32)),
    ("idb", pltpu.VMEM((TOPC, MROWS, 128), F32)),
    ("raw", pltpu.VMEM((MROWS, VOCAB), F32)),
    ("cols", pltpu.VMEM((384, 128), F32)),
    ("sbuf", pltpu.VMEM((8, 16, 384), BF16)),
    ("ss", pltpu.SemaphoreType.DMA),
    ("sr", pltpu.SemaphoreType.DMA),
    ("gbuf", pltpu.VMEM((CHIPS, 16, 384), BF16)),
    ("gs", pltpu.SemaphoreType.DMA),
    ("gr", pltpu.SemaphoreType.DMA),
)


class Refs:
    pass


def kernel(
    hidden, medusa_w, embedding, cand_ids, tree_q, tree_kv, prompt_kv,
    block_group, block_len, block_empty, parents, out_weight, post_gain, resid,
    out_ref, stat_ref, *scratch
):
    s = Refs()
    for (name, _), ref in zip(SCRATCH, scratch):
        setattr(s, name, ref)
    me = lax.axis_index("blk")
    mz = lax.axis_index("mp")
    chip, mc = me // 2, me % 2
    mx, my = chip // 4, chip % 4
    sibling = me + 1 - 2 * mc
    head, part = me // 8, me % 8

    def peer_of(step):
        return lax.rem(me + step, NB)

    def chip_of(step):
        return lax.rem(chip + step, CHIPS)

    def z_of(step):
        return lax.rem(mz + step, 4)

    def remote(src, dst, ss, rs, **where):
        return pltpu.make_async_remote_copy(
            src_ref=src, dst_ref=dst, send_sem=ss, recv_sem=rs,
            device_id=where, device_id_type=MESH,
        )

    def drain(ref, sem):
        pltpu.make_async_copy(ref, ref, sem).wait()

    inputs = []

    def fetch(src, dst):
        copy = pltpu.make_async_copy(src, dst, s.sem_in.at[len(inputs)])
        copy.start()
        inputs.append(copy)
        return copy

    first = DEPTH * me
    start = jnp.minimum((first // 128) * 128, D - 256)
    start = pl.multiple_of(start, 128)
    shift = pl.multiple_of(first - start, 16)
    for m in range(2):
        s.wpad[m] = jnp.zeros((256, UNITS), BF16)
    in_w = [
        fetch(hidden.at[:, pl.ds(start, 256)], s.hwin),
        fetch(medusa_w.at[0], s.wpad.at[0, pl.ds(shift, DEPTH), :]),
        fetch(medusa_w.at[1], s.wpad.at[1, pl.ds(shift, DEPTH), :]),
    ]
    in_q = fetch(tree_q, s.qbuf)
    in_k = fetch(prompt_kv.at[0, 0], s.kbuf)
    in_v = fetch(prompt_kv.at[1, 0], s.vbuf)
    in_h = []
    for p in range(2):
        chunk = 2 * me + p
        rblk, lane = chunk // 7, chunk % 7
        col = pl.multiple_of(mz * UNITS + lane * 128, 128)
        for half in range(2):
            row = pl.multiple_of(((rblk * 2 + half) % 9) * 16, 16)
            in_h.append(
                fetch(
                    hidden.at[pl.ds(row, 16), pl.ds(col, 128)],
                    s.hown.at[p, pl.ds(half * 16, 16), :],
                )
            )
    qcol = pl.multiple_of(head * HEAD, HEAD)
    kcol = pl.multiple_of((head // 2) * HEAD, HEAD)
    in_t = [
        fetch(tree_q.at[:, :, pl.ds(qcol, HEAD)], s.tqb.at[:, pl.ds(0, TREE), :]),
        fetch(tree_kv.at[0, :, :, pl.ds(kcol, HEAD)], s.tkb.at[:, pl.ds(0, TREE), :]),
        fetch(tree_kv.at[1, :, :, pl.ds(kcol, HEAD)], s.tvb.at[:, pl.ds(0, TREE), :]),
        fetch(parents, s.parv),
    ]
    in_c = fetch(cand_ids, s.candv)
    in_o = fetch(out_weight, s.outv)
    in_g = [fetch(post_gain, s.gainv), fetch(resid, s.residv)]
    in_e = fetch(embedding, s.embv)

    barrier = pltpu.get_barrier_semaphore()

    def greet(step, carry):
        pl.semaphore_signal(
            barrier, inc=1, device_id={"blk": peer_of(step)}, device_id_type=MESH
        )
        return carry

    lax.fori_loop(1, NB, greet, 0)
    for step in range(1, 4):
        pl.semaphore_signal(
            barrier, inc=1, device_id={"mp": z_of(step)}, device_id_type=MESH
        )
        pl.semaphore_signal(
            barrier, inc=1, device_id={"blk": sibling, "mp": z_of(step)}, device_id_type=MESH
        )

    for copy in in_w:
        copy.wait()
    hwin = s.hwin[...]
    for m in range(2):
        product = dot(hwin, s.wpad[m]).astype(BF16)
        for u in range(9):
            unit = m * 9 + u
            for lane in range(7):
                chunk = (unit // 2) * 7 + lane
                low = (unit % 2) * 16
                s.pbuf[chunk // 4, chunk // 2 % 2, chunk % 2, low:low + 16, :] = (
                    product[u * 16:u * 16 + 16, lane * 128:lane * 128 + 128]
                )
    s.pbuf[CHIPS - 1, 1, 1] = jnp.zeros((32, 128), BF16)
    pl.semaphore_wait(barrier, NB - 1 + 6)
    remote(s.pbuf.at[:, 1 - mc], s.psib, s.pc_s, s.pc_r, blk=sibling).start()
    drain(s.psib, s.pc_r)
    s.psum[...] = (s.pbuf[:, mc].astype(F32) + s.psib[...].astype(F32)).astype(BF16)

    def send_product(step, carry):
        to = chip_of(step)
        remote(s.psum.at[to], s.precv.at[step - 1], s.ps, s.pr, blk=2 * to + mc).start()
        return carry

    lax.fori_loop(1, CHIPS, send_product, 0)

    group = block_group[0]
    limit = jnp.where(block_empty[0] == 0, block_len[0], 0)
    spread = (
        (iota((64, TREE), 0) // 8) * 6 + iota((64, TREE), 0) % 8 == iota((64, TREE), 1)
    ) & (iota((64, TREE), 0) % 8 < 6)
    spread = spread.astype(F32).astype(BF16)
    in_q.wait()
    queries = dot(spread, s.qbuf[group]).astype(BF16)
    in_k.wait()
    in_v.wait()
    row8 = iota((8, HEAD), 0)
    row_l = iota((8, 128), 0)
    lane_l = iota((8, 128), 1)
    tag = jnp.full((8, HEAD), group, jnp.int32).astype(F32)
    for kv in range(2):
        cols = slice(kv * HEAD, kv * HEAD + HEAD)
        two = jnp.concatenate(
            [queries[:, (2 * kv + r) * HEAD:(2 * kv + r + 1) * HEAD] for r in range(2)], 0
        )
        numer = jnp.zeros((128, HEAD), F32)
        denom = jnp.zeros((128, 128), F32)
        for tile in range(SLOTS // KEY_TILE):
            keys = slice(tile * KEY_TILE, tile * KEY_TILE + KEY_TILE)
            seen = iota((128, KEY_TILE), 1) + tile * KEY_TILE < limit
            weight = jnp.where(seen, weigh(dot(two, s.kbuf[keys, cols], NT)), 0.0)
            for piece in range(KEY_TILE // 128):
                denom = denom + weight[:, piece * 128:piece * 128 + 128]
            numer = numer + dot(weight.astype(BF16), s.vbuf[keys, cols])
        total = jnp.broadcast_to(jnp.sum(denom, 1, keepdims=True), (128, 128))
        high = total.astype(BF16).astype(F32)
        rest = total - high
        for r in range(2):
            for q in range(8):
                rows = slice(r * 64 + q * 8, r * 64 + q * 8 + 8)
                spots = jnp.where(lane_l == row_l, high[rows], 0.0) + jnp.where(
                    lane_l == row_l + 8, rest[rows], 0.0
                )
                spots = jnp.sum(jnp.where(row_l < 6, spots, 0.0), 0, keepdims=True)
                spots = jnp.concatenate([spots, jnp.zeros((1, 128), F32)], 1)
                piece = jnp.where(row8 < 6, numer[rows], jnp.where(row8 == 6, spots, tag))
                s.abuf[(2 * kv + r) * 8 + q] = piece.astype(BF16)

    def send_attention(step, carry):
        peer = peer_of(step)
        remote(s.abuf.at[peer], s.arecv.at[step], s.as_, s.ar, blk=peer).start()
        return carry

    lax.fori_loop(1, NB, send_attention, 0)
    s.arecv[0] = s.abuf[me]

    for copy in in_h:
        copy.wait()
    drain(s.precv, s.pr)
    inner = lax.fori_loop(
        0, CHIPS - 1,
        lambda i, acc: acc + s.precv[i].astype(F32),
        s.psum[chip].astype(F32),
    )
    fresh = (s.hown[...].astype(F32) + inner / (1.0 + jnp.exp(-inner))).astype(BF16)
    s.f0[my, mc, mx, mz] = fresh[0]
    s.f1[mx, mc, my, mz] = fresh[1]
    for step in range(1, 4):
        for which, own in enumerate((s.f0.at[my, mc, mx, mz], s.f1.at[mx, mc, my, mz])):
            remote(own, own, s.fz_s.at[which], s.fz_r.at[which], mp=z_of(step)).start()

    for copy in in_t:
        copy.wait()
    for buf in (s.tqb, s.tkb, s.tvb):
        for g in range(GROUPS):
            buf[g, TREE:64, :] = jnp.zeros((64 - TREE, HEAD), BF16)
    place = (iota((TREE, 256), 0) == iota((TREE, 256), 1) % 64).astype(F32).astype(BF16)
    spots = dot(s.parv[...].astype(F32).astype(BF16), place)
    sub = iota((256, 256), 0)
    lan = iota((256, 256), 1)
    eye = sub == lan
    pick_row = iota((32, 256), 0)
    pick_col = iota((32, 256), 1)
    pick = (pick_col == (pick_row // 8) * 64 + part * 6 + pick_row % 8) & (pick_row % 8 < 6)
    pick = pick.astype(F32).astype(BF16)
    for b in range(3):
        mine = iota((GROUPS, 256), 0) == 4 * b + iota((GROUPS, 256), 1) // 64
        parent = jnp.sum(jnp.where(mine, spots, 0.0), 0, keepdims=True)
        wanted = parent + (iota((1, 256), 1) // 64 * 64).astype(F32)
        linked = (sub.astype(F32) == wanted) & (lan % 64 > 0)
        reach = jnp.where(eye | linked, 1.0, 0.0).astype(BF16)
        for sweep in range(6):
            reach = jnp.minimum(dot(reach, reach), 1.0).astype(BF16)
        mask = dot(pick, reach, NT)
        tq = s.tqb[4 * b:4 * b + 4].reshape(256, HEAD)
        tk = s.tkb[4 * b:4 * b + 4].reshape(256, HEAD)
        tv = s.tvb[4 * b:4 * b + 4].reshape(256, HEAD)
        rows = dot(pick, tq).astype(BF16)
        weight = weigh(dot(rows, tk, NT)) * mask
        numer = dot(weight.astype(BF16), tv)
        denom = jnp.broadcast_to(jnp.sum(weight, 1, keepdims=True), (32, 128))
        s.treen[4 * b:4 * b + 4] = numer.reshape(4, 8, HEAD)
        s.treed[4 * b:4 * b + 4] = denom.reshape(4, 8, 128)

    def x_peer(step):
        return lax.rem(mx + step, 4) * 8 + my * 2 + mc

    def y_peer(step):
        return mx * 8 + lax.rem(my + step, 4) * 2 + mc

    lines = ((s.f0, my, mx, x_peer, y_peer), (s.f1, mx, my, y_peer, x_peer))
    def pass_on(which, block, far):
        for step in range(1, 4):
            remote(
                block, block, s.fb_s.at[which], s.fb_r.at[which, step - 1], blk=far(step)
            ).start()
        remote(block, block, s.fc_s.at[which], s.fc_r.at[which], blk=sibling).start()

    for which, (buf, slow, quick, near, far) in enumerate(lines):
        drain(buf.at[slow, mc, quick, pl.ds(0, 3)], s.fz_r.at[which])
        own = buf.at[slow, mc, quick]
        for step in range(1, 4):
            remote(
                own, own, s.fa_s.at[which], s.fa_r.at[which, step - 1], blk=near(step)
            ).start()
    for which, (buf, slow, quick, near, far) in enumerate(lines):
        pass_on(which, buf.at[slow, mc, quick], far)

    drain(s.arecv.at[pl.ds(1, NB - 1)], s.ar)
    for half in range(2):
        def add(i, carry):
            got = s.arecv[i].astype(F32)
            named = jnp.broadcast_to(got[7:8], (8, HEAD))
            return tuple(
                acc + jnp.where(named == float(half * 6 + g), got, 0.0)
                for g, acc in enumerate(carry)
            )

        sums = lax.fori_loop(0, NB, add, (jnp.zeros((8, HEAD), F32),) * 6)
        for g in range(6):
            spots = jnp.broadcast_to(sums[g][6:7, :128], (8, 128))
            spots = jnp.where((lane_l == row_l) | (lane_l == row_l + 8), spots, 0.0)
            denom = jnp.sum(spots, 1, keepdims=True) + s.treed[half * 6 + g][:, :1]
            denom = jnp.where(iota((8, 1), 0) < 6, denom, 1.0)
            numer = sums[g] + s.treen[half * 6 + g]
            numer = jnp.where(row8 < 6, numer, 0.0)
            s.hbuf[half * 6 + g] = (numer / denom).astype(BF16)

    def heads_copy(g):
        chunk = g * 8 + part
        owner = chunk // 3
        spot = (chunk % 3) * 4 + head
        return owner, spot

    def send_heads(g, carry):
        owner, spot = heads_copy(g)

        @pl.when(owner != me)
        def _():
            remote(
                s.hbuf.at[g], s.hrecv.at[spot], s.hs.at[g], s.hr, blk=owner
            ).start()

        @pl.when(owner == me)
        def _():
            pltpu.make_async_copy(s.hbuf.at[g], s.hrecv.at[spot], s.hr).start()

        return carry

    lax.fori_loop(0, GROUPS, send_heads, 0)

    for step in range(1, 4):
        for which, (buf, slow, quick, near, far) in enumerate(lines):
            came = buf.at[slow, mc, lax.rem(quick - step + 4, 4)]
            drain(came, s.fa_r.at[which, step - 1])
            pass_on(which, came, far)

    in_o.wait()
    drain(s.hrecv, s.hr)
    lhs = jnp.concatenate(
        [
            jnp.concatenate([s.hrecv[t * 4 + h].astype(F32) for h in range(HEADS)], 1)
            for t in range(3)
        ],
        0,
    ).astype(BF16)
    for tile in range(7):
        cols = slice(tile * 512, tile * 512 + 512)
        got = dot(lhs, s.outv[:, cols]).astype(BF16)
        s.zbuf[mz, :, :, cols] = got.reshape(3, 8, 512)
    for step in range(1, 4):
        own = s.zbuf.at[mz]
        remote(own, own, s.zs, s.zr, mp=z_of(step)).start()

    in_c.wait()
    s.idv[...] = jnp.zeros((2, 16, 384), F32)
    for m in range(2):
        s.idv[m, 0:TOPC, 0:ROWS] = s.candv[:, m, :].astype(F32)
    ids = s.idv[0] + pltpu.roll(s.idv[1], ROWS, 1)
    base = ((me * 4 + mz) * VOCAB).astype(F32)
    ids = jnp.concatenate([ids - base, jnp.zeros((112, 384), F32)], 0).T
    for c in range(TOPC):
        s.idb[c] = jnp.broadcast_to(ids[:MROWS, c:c + 1], (MROWS, 128))

    for step in range(1, 4):
        for which, (buf, slow, quick, near, far) in enumerate(lines):
            came = buf.at[lax.rem(slow - step + 4, 4), mc]
            drain(came, s.fb_r.at[which, step - 1])
            remote(came, came, s.fc_s.at[which], s.fc_r.at[which], blk=sibling).start()

    def arrange(core):
        def body(one, carry):
            x, y = one // 4, one % 4
            for p in range(2):
                chunk = 4 * one + 2 * core + p
                row = pl.multiple_of((chunk // 7) * 32, 32)

                @pl.when(chunk < 63)
                def _():
                    for z in range(4):
                        col = pl.multiple_of(z * UNITS + (chunk % 7) * 128, 128)
                        piece = s.f0[y, core, x, z] if p == 0 else s.f1[x, core, y, z]
                        s.fresh[pl.ds(row, 32), pl.ds(col, 128)] = piece

            return carry

        lax.fori_loop(0, CHIPS, body, 0)

    arrange(mc)
    for which, (buf, slow, quick, near, far) in enumerate(lines):
        drain(buf.at[pl.ds(0, 2)], s.fc_r.at[which])
    arrange(1 - mc)

    in_e.wait()
    s.raw[...] = dot(s.fresh[...], s.embv[...], NT)
    lane = iota((16, 128), 1)
    spot = [lane.astype(F32) + 128.0 * k for k in range(VOCAB // 128)]

    def score(part, carry):
        rows = pl.ds(pl.multiple_of(part * 16, 16), 16)
        total = jnp.zeros((16, 128), F32)
        picks = [jnp.zeros((16, 128), F32)] * TOPC
        named = [s.idb[c, rows, :] for c in range(TOPC)]
        for k in range(VOCAB // 128):
            logits = 30.0 * jnp.tanh(s.raw[rows, k * 128:k * 128 + 128] * (1.0 / 30.0))
            total = total + jnp.exp(logits)
            picks = [jnp.where(named[c] == spot[k], logits, picks[c]) for c in range(TOPC)]
        found = jnp.where(lane == TOPC, jnp.sum(total, 1, keepdims=True), 0.0)
        for c in range(TOPC):
            found = found + jnp.where(lane == c, jnp.sum(picks[c], 1, keepdims=True), 0.0)
        s.cols[rows, :] = found
        return carry

    s.cols[MROWS:, :] = jnp.zeros((384 - MROWS, 128), F32)
    lax.fori_loop(0, MROWS // 16, score, 0)
    stats = s.cols[...].T[:16]
    tall = iota((16, 384), 0)

    def pack(stats):
        total = stats[TOPC:TOPC + 1]
        high = total.astype(BF16).astype(F32)
        middle = (total - high).astype(BF16).astype(F32)
        low = total - high - middle
        stats = jnp.where(tall == TOPC, high, stats)
        stats = jnp.where(tall == TOPC + 1, middle, stats)
        return jnp.where(tall == TOPC + 2, low, stats).astype(BF16)

    def unpack(parts):
        stats = parts[0].astype(F32)
        for more in parts[1:]:
            stats = stats + more.astype(F32)
        total = stats[TOPC:TOPC + 1] + stats[TOPC + 1:TOPC + 2] + stats[TOPC + 2:TOPC + 3]
        return jnp.where(tall == TOPC, total, stats)

    def share(buf, spot, sems, targets):
        own = buf.at[spot]
        for where in targets:
            remote(own, own, *sems, **where).start()

    s.sbuf[mz * 2 + mc] = pack(stats)
    targets = [{"blk": sibling}]
    for step in range(1, 4):
        targets += [{"mp": z_of(step)}, {"blk": sibling, "mp": z_of(step)}]
    share(s.sbuf, mz * 2 + mc, (s.ss, s.sr), targets)

    for copy in in_g:
        copy.wait()
    drain(s.zbuf.at[pl.ds(0, 3)], s.zr)
    attn = s.zbuf[0].astype(F32)
    for z in range(1, 4):
        attn = attn + s.zbuf[z].astype(F32)
    mean = jnp.sum(attn * attn, -1, keepdims=True) * (1.0 / D)
    normed = attn * lax.rsqrt(mean + 1e-06) * s.gainv[...].reshape(1, 1, D)
    for t in range(3):
        s.nrm[6 * t:6 * t + 6, :] = normed[t, :6]
    out_ref[...] = (s.nrm[0:18, :] + s.residv[...].astype(F32)).astype(BF16)

    drain(s.sbuf.at[pl.ds(0, 7)], s.sr)
    s.gbuf[chip] = pack(unpack([s.sbuf[i] for i in range(8)]))
    share(
        s.gbuf, chip, (s.gs, s.gr),
        [{"blk": 2 * chip_of(step) + mc} for step in range(1, CHIPS)],
    )
    drain(s.gbuf.at[pl.ds(0, CHIPS - 1)], s.gr)
    full = unpack([s.gbuf[i] for i in range(CHIPS)])
    found = full - jnp.log(full[TOPC:TOPC + 1])
    stat_ref[:, 0, :] = found[:TOPC, :ROWS]
    stat_ref[:, 1, :] = pltpu.roll(found, 384 - ROWS, 1)[:TOPC, :ROWS]

    drain(s.psib, s.pc_s)
    drain(s.precv, s.ps)
    drain(s.arecv.at[pl.ds(1, NB - 1)], s.as_)
    for which, (buf, slow, quick, near, far) in enumerate(lines):
        drain(buf.at[slow, mc, quick, pl.ds(0, 3)], s.fz_s.at[which])
        drain(buf.at[slow, mc, pl.ds(0, 3)], s.fa_s.at[which])
        drain(buf.at[pl.ds(0, 3), mc], s.fb_s.at[which])
        drain(buf.at[pl.ds(0, 2)], s.fc_s.at[which])

    def sent_heads(g, carry):
        owner, spot = heads_copy(g)

        @pl.when(owner != me)
        def _():
            drain(s.hbuf.at[g], s.hs.at[g])

        return carry

    lax.fori_loop(0, GROUPS, sent_heads, 0)
    drain(s.zbuf.at[pl.ds(0, 3)], s.zs)
    drain(s.sbuf.at[pl.ds(0, 7)], s.ss)
    drain(s.gbuf.at[pl.ds(0, CHIPS - 1)], s.gs)


def per_device(
    hidden, medusa_w, embedding, cand_ids, tree_q, tree_key_value, prompt_key_value,
    block_group, block_len, block_empty, parents, out_weight, post_gain, resid,
):
    anywhere = pl.BlockSpec(memory_space=pl.ANY)
    scalar = pl.BlockSpec(memory_space=pltpu.SMEM)
    whole = pl.BlockSpec(memory_space=pltpu.VMEM)
    layer_out, stats = pl.pallas_call(
        kernel,
        out_shape=(
            jax.ShapeDtypeStruct((18, D), BF16),
            jax.ShapeDtypeStruct((TOPC, 2, ROWS), F32),
        ),
        in_specs=[anywhere] * 7 + [scalar] * 3 + [anywhere] * 4,
        out_specs=(whole, whole),
        scratch_shapes=[kind for _, kind in SCRATCH],
        compiler_params=pltpu.CompilerParams(
            collective_id=0, has_side_effects=True, vmem_limit_bytes=60 << 20
        ),
    )(
        hidden, medusa_w, embedding, cand_ids.transpose(2, 0, 1), tree_q, tree_key_value,
        prompt_key_value, block_group, block_len, block_empty, parents, out_weight,
        post_gain, resid,
    )
    return (stats.transpose(1, 2, 0), layer_out)


def solution(mesh):
    placed = (
        P(),
        P(None, "blk", "mp"),
        P(("blk", "mp"), None),
        P(),
        P(None, None, "mp"),
        P(None, None, None, "mp"),
        P(None, "blk", None, "mp"),
        P("blk"),
        P("blk"),
        P("blk"),
        P(),
        P("mp", None),
        P(),
        P("blk", None),
    )
    return jax.shard_map(
        per_device, mesh=mesh, in_specs=placed, out_specs=(P(), P("blk", None)), check_vma=False
    )
```

```python
import jax
import jax.numpy as jnp
from jax import lax
from jax.experimental import pallas as pl
from jax.experimental.pallas import tpu as pltpu
from jax.sharding import PartitionSpec as P

MESH = pl.DeviceIdType.MESH
F32 = jnp.float32
BF16 = jnp.bfloat16

D = 3584
ROWS = 144
MROWS = 288
UNITS = 896
DEPTH = 112
GROUPS = 12
TREE = 48
HEAD = 256
HEADS = 4
SLOTS = 2048
VOCAB = 1024
TOPC = 10
NB = 32
CHIPS = 16
KEY_TILE = 512
NT = (((1,), (1,)), ((), ()))
NN = (((1,), (0,)), ((), ()))


def dot(a, b, dims=NN):
    return lax.dot_general(a, b, dims, preferred_element_type=F32)


def iota(shape, axis):
    return lax.broadcasted_iota(jnp.int32, shape, axis)


def weigh(scores):
    return jnp.exp(50.0 * jnp.tanh(scores * (HEAD ** (-0.5) / 50.0)))


SCRATCH = (
    ("hwin", pltpu.VMEM((ROWS, 256), BF16)),
    ("wpad", pltpu.VMEM((2, 256, UNITS), BF16)),
    ("hown", pltpu.VMEM((2, 32, 128), BF16)),
    ("embv", pltpu.VMEM((VOCAB, D), BF16)),
    ("outv", pltpu.VMEM((HEADS * HEAD, D), BF16)),
    ("kbuf", pltpu.VMEM((SLOTS, 512), BF16)),
    ("vbuf", pltpu.VMEM((SLOTS, 512), BF16)),
    ("qbuf", pltpu.VMEM((GROUPS, TREE, 1024), BF16)),
    ("tqb", pltpu.VMEM((GROUPS, 64, HEAD), BF16)),
    ("tkb", pltpu.VMEM((GROUPS, 64, HEAD), BF16)),
    ("tvb", pltpu.VMEM((GROUPS, 64, HEAD), BF16)),
    ("candv", pltpu.VMEM((TOPC, 2, ROWS), jnp.int32)),
    ("parv", pltpu.VMEM((GROUPS, TREE), jnp.int32)),
    ("gainv", pltpu.VMEM((D,), F32)),
    ("residv", pltpu.VMEM((18, D), BF16)),
    ("sem_in", pltpu.SemaphoreType.DMA((20,))),
    ("pbuf", pltpu.VMEM((CHIPS, 2, 2, 32, 128), BF16)),
    ("psib", pltpu.VMEM((CHIPS, 2, 32, 128), BF16)),
    ("psum", pltpu.VMEM((CHIPS, 2, 32, 128), BF16)),
    ("precv", pltpu.VMEM((CHIPS - 1, 2, 32, 128), BF16)),
    ("pc_s", pltpu.SemaphoreType.DMA),
    ("pc_r", pltpu.SemaphoreType.DMA),
    ("ps", pltpu.SemaphoreType.DMA),
    ("pr", pltpu.SemaphoreType.DMA),
    ("f0", pltpu.VMEM((4, 2, 4, 4, 32, 128), BF16)),
    ("f1", pltpu.VMEM((4, 2, 4, 4, 32, 128), BF16)),
    ("fz_s", pltpu.SemaphoreType.DMA((2,))),
    ("fz_r", pltpu.SemaphoreType.DMA((2,))),
    ("fa_s", pltpu.SemaphoreType.DMA((2,))),
    ("fa_r", pltpu.SemaphoreType.DMA((2, 3))),
    ("fb_s", pltpu.SemaphoreType.DMA((2,))),
    ("fb_r", pltpu.SemaphoreType.DMA((2, 3, 4))),
    ("fc_s", pltpu.SemaphoreType.DMA((2,))),
    ("fc_r", pltpu.SemaphoreType.DMA((2,))),
    ("fresh", pltpu.VMEM((MROWS, D), BF16)),
    ("abuf", pltpu.VMEM((NB, 8, HEAD), BF16)),
    ("arecv", pltpu.VMEM((NB, 8, HEAD), BF16)),
    ("as_", pltpu.SemaphoreType.DMA),
    ("ar", pltpu.SemaphoreType.DMA),
    ("treen", pltpu.VMEM((GROUPS, 8, HEAD), F32)),
    ("treed", pltpu.VMEM((GROUPS, 8, 128), F32)),
    ("hbuf", pltpu.VMEM((GROUPS, 8, HEAD), BF16)),
    ("hrecv", pltpu.VMEM((GROUPS, 8, HEAD), BF16)),
    ("hs", pltpu.SemaphoreType.DMA((GROUPS,))),
    ("hr", pltpu.SemaphoreType.DMA),
    ("zbuf", pltpu.VMEM((4, 3, 8, D), BF16)),
    ("zs", pltpu.SemaphoreType.DMA),
    ("zr", pltpu.SemaphoreType.DMA),
    ("nrm", pltpu.VMEM((24, D), F32)),
    ("layer", pltpu.VMEM((18, D), BF16)),
    ("sem_out", pltpu.SemaphoreType.DMA),
    ("idv", pltpu.VMEM((2, 16, 384), F32)),
    ("idb", pltpu.VMEM((TOPC, MROWS, 128), F32)),
    ("tally", pltpu.VMEM((TOPC + 1, MROWS, 128), F32)),
    ("cols", pltpu.VMEM((384, 128), F32)),
    ("sbuf", pltpu.VMEM((8, 16, 384), BF16)),
    ("ss", pltpu.SemaphoreType.DMA),
    ("sr", pltpu.SemaphoreType.DMA),
    ("gbuf", pltpu.VMEM((CHIPS, 16, 384), BF16)),
    ("gs", pltpu.SemaphoreType.DMA),
    ("gr", pltpu.SemaphoreType.DMA),
)


class Refs:
    pass


def kernel(
    hidden, medusa_w, embedding, cand_ids, tree_q, tree_kv, prompt_kv,
    block_group, block_len, block_empty, parents, out_weight, post_gain, resid,
    out_ref, stat_ref, *scratch
):
    s = Refs()
    for (name, _), ref in zip(SCRATCH, scratch):
        setattr(s, name, ref)
    me = lax.axis_index("blk")
    mz = lax.axis_index("mp")
    chip, mc = me // 2, me % 2
    mx, my = chip // 4, chip % 4
    sibling = me + 1 - 2 * mc
    head, part = me // 8, me % 8

    def peer_of(step):
        return lax.rem(me + step, NB)

    def chip_of(step):
        return lax.rem(chip + step, CHIPS)

    def z_of(step):
        return lax.rem(mz + step, 4)

    def x_peer(step):
        return lax.rem(mx + step, 4) * 8 + my * 2 + mc

    def y_peer(step):
        return mx * 8 + lax.rem(my + step, 4) * 2 + mc

    def remote(src, dst, ss, rs, **where):
        return pltpu.make_async_remote_copy(
            src_ref=src, dst_ref=dst, send_sem=ss, recv_sem=rs,
            device_id=where, device_id_type=MESH,
        )

    def drain(ref, sem):
        pltpu.make_async_copy(ref, ref, sem).wait()

    inputs = []

    def fetch(src, dst):
        copy = pltpu.make_async_copy(src, dst, s.sem_in.at[len(inputs)])
        copy.start()
        inputs.append(copy)
        return copy

    first = DEPTH * me
    start = jnp.minimum((first // 128) * 128, D - 256)
    start = pl.multiple_of(start, 128)
    shift = pl.multiple_of(first - start, 16)
    for m in range(2):
        s.wpad[m] = jnp.zeros((256, UNITS), BF16)
    in_w = [
        fetch(hidden.at[:, pl.ds(start, 256)], s.hwin),
        fetch(medusa_w.at[0], s.wpad.at[0, pl.ds(shift, DEPTH), :]),
        fetch(medusa_w.at[1], s.wpad.at[1, pl.ds(shift, DEPTH), :]),
    ]
    in_q = fetch(tree_q, s.qbuf)
    in_k = fetch(prompt_kv.at[0, 0], s.kbuf)
    in_v = fetch(prompt_kv.at[1, 0], s.vbuf)
    in_h = []
    for p in range(2):
        chunk = 2 * me + p
        rblk, lane = chunk // 7, chunk % 7
        col = pl.multiple_of(mz * UNITS + lane * 128, 128)
        for half in range(2):
            row = pl.multiple_of(((rblk * 2 + half) % 9) * 16, 16)
            in_h.append(
                fetch(
                    hidden.at[pl.ds(row, 16), pl.ds(col, 128)],
                    s.hown.at[p, pl.ds(half * 16, 16), :],
                )
            )
    qcol = pl.multiple_of(head * HEAD, HEAD)
    kcol = pl.multiple_of((head // 2) * HEAD, HEAD)
    in_t = [
        fetch(tree_q.at[:, :, pl.ds(qcol, HEAD)], s.tqb.at[:, pl.ds(0, TREE), :]),
        fetch(tree_kv.at[0, :, :, pl.ds(kcol, HEAD)], s.tkb.at[:, pl.ds(0, TREE), :]),
        fetch(tree_kv.at[1, :, :, pl.ds(kcol, HEAD)], s.tvb.at[:, pl.ds(0, TREE), :]),
        fetch(parents, s.parv),
    ]
    in_c = fetch(cand_ids, s.candv)
    in_o = fetch(out_weight, s.outv)
    in_g = [fetch(post_gain, s.gainv), fetch(resid, s.residv)]
    in_e = fetch(embedding, s.embv)

    barrier = pltpu.get_barrier_semaphore()

    def greet(step, carry):
        pl.semaphore_signal(
            barrier, inc=1, device_id={"blk": peer_of(step)}, device_id_type=MESH
        )
        return carry

    lax.fori_loop(1, NB, greet, 0)
    for step in range(1, 4):
        pl.semaphore_signal(
            barrier, inc=1, device_id={"mp": z_of(step)}, device_id_type=MESH
        )
        pl.semaphore_signal(
            barrier, inc=1, device_id={"blk": sibling, "mp": z_of(step)}, device_id_type=MESH
        )

    for up in range(1, 4):
        for step in range(1, 4):
            for peer in (x_peer(step), y_peer(step)):
                pl.semaphore_signal(
                    barrier, inc=1, device_id={"blk": peer, "mp": z_of(up)},
                    device_id_type=MESH,
                )

    for copy in in_w:
        copy.wait()
    hwin = s.hwin[...]
    for m in range(2):
        product = dot(hwin, s.wpad[m]).astype(BF16)
        for u in range(9):
            unit = m * 9 + u
            for lane in range(7):
                chunk = (unit // 2) * 7 + lane
                low = (unit % 2) * 16
                s.pbuf[chunk // 4, chunk // 2 % 2, chunk % 2, low:low + 16, :] = (
                    product[u * 16:u * 16 + 16, lane * 128:lane * 128 + 128]
                )
    s.pbuf[CHIPS - 1, 1, 1] = jnp.zeros((32, 128), BF16)
    pl.semaphore_wait(barrier, NB - 1 + 6 + 18)
    remote(s.pbuf.at[:, 1 - mc], s.psib, s.pc_s, s.pc_r, blk=sibling).start()
    drain(s.psib, s.pc_r)
    s.psum[...] = (s.pbuf[:, mc].astype(F32) + s.psib[...].astype(F32)).astype(BF16)

    def send_product(step, carry):
        to = chip_of(step)
        remote(s.psum.at[to], s.precv.at[step - 1], s.ps, s.pr, blk=2 * to + mc).start()
        return carry

    lax.fori_loop(1, CHIPS, send_product, 0)

    group = block_group[0]
    limit = jnp.where(block_empty[0] == 0, block_len[0], 0)
    spread = (
        (iota((64, TREE), 0) // 8) * 6 + iota((64, TREE), 0) % 8 == iota((64, TREE), 1)
    ) & (iota((64, TREE), 0) % 8 < 6)
    spread = spread.astype(F32).astype(BF16)
    in_q.wait()
    queries = dot(spread, s.qbuf[group]).astype(BF16)
    in_k.wait()
    in_v.wait()
    row8 = iota((8, HEAD), 0)
    row_l = iota((8, 128), 0)
    lane_l = iota((8, 128), 1)
    tag = jnp.full((8, HEAD), group, jnp.int32).astype(F32)
    for kv in range(2):
        cols = slice(kv * HEAD, kv * HEAD + HEAD)
        two = jnp.concatenate(
            [queries[:, (2 * kv + r) * HEAD:(2 * kv + r + 1) * HEAD] for r in range(2)], 0
        )
        numer = jnp.zeros((128, HEAD), F32)
        denom = jnp.zeros((128, 128), F32)
        for tile in range(SLOTS // KEY_TILE):
            keys = slice(tile * KEY_TILE, tile * KEY_TILE + KEY_TILE)
            seen = iota((128, KEY_TILE), 1) + tile * KEY_TILE < limit
            weight = jnp.where(seen, weigh(dot(two, s.kbuf[keys, cols], NT)), 0.0)
            for piece in range(KEY_TILE // 128):
                denom = denom + weight[:, piece * 128:piece * 128 + 128]
            numer = numer + dot(weight.astype(BF16), s.vbuf[keys, cols])
        total = jnp.broadcast_to(jnp.sum(denom, 1, keepdims=True), (128, 128))
        high = total.astype(BF16).astype(F32)
        rest = total - high
        for r in range(2):
            for q in range(8):
                rows = slice(r * 64 + q * 8, r * 64 + q * 8 + 8)
                spots = jnp.where(lane_l == row_l, high[rows], 0.0) + jnp.where(
                    lane_l == row_l + 8, rest[rows], 0.0
                )
                spots = jnp.sum(jnp.where(row_l < 6, spots, 0.0), 0, keepdims=True)
                spots = jnp.concatenate([spots, jnp.zeros((1, 128), F32)], 1)
                piece = jnp.where(row8 < 6, numer[rows], jnp.where(row8 == 6, spots, tag))
                s.abuf[(2 * kv + r) * 8 + q] = piece.astype(BF16)

    def send_attention(step, carry):
        peer = peer_of(step)
        remote(s.abuf.at[peer], s.arecv.at[step], s.as_, s.ar, blk=peer).start()
        return carry

    lax.fori_loop(1, NB, send_attention, 0)
    s.arecv[0] = s.abuf[me]

    for copy in in_t:
        copy.wait()
    for buf in (s.tqb, s.tkb, s.tvb):
        for g in range(GROUPS):
            buf[g, TREE:64, :] = jnp.zeros((64 - TREE, HEAD), BF16)
    place = (iota((TREE, 256), 0) == iota((TREE, 256), 1) % 64).astype(F32).astype(BF16)
    spots = dot(s.parv[...].astype(F32).astype(BF16), place)
    sub = iota((256, 256), 0)
    lan = iota((256, 256), 1)
    eye = sub == lan
    pick_row = iota((32, 256), 0)
    pick_col = iota((32, 256), 1)
    pick = (pick_col == (pick_row // 8) * 64 + part * 6 + pick_row % 8) & (pick_row % 8 < 6)
    pick = pick.astype(F32).astype(BF16)
    for b in range(3):
        mine = iota((GROUPS, 256), 0) == 4 * b + iota((GROUPS, 256), 1) // 64
        parent = jnp.sum(jnp.where(mine, spots, 0.0), 0, keepdims=True)
        wanted = parent + (iota((1, 256), 1) // 64 * 64).astype(F32)
        linked = (sub.astype(F32) == wanted) & (lan % 64 > 0)
        reach = jnp.where(eye | linked, 1.0, 0.0).astype(BF16)
        for sweep in range(6):
            reach = jnp.minimum(dot(reach, reach), 1.0).astype(BF16)
        mask = dot(pick, reach, NT)
        tq = s.tqb[4 * b:4 * b + 4].reshape(256, HEAD)
        tk = s.tkb[4 * b:4 * b + 4].reshape(256, HEAD)
        tv = s.tvb[4 * b:4 * b + 4].reshape(256, HEAD)
        rows = dot(pick, tq).astype(BF16)
        weight = weigh(dot(rows, tk, NT)) * mask
        numer = dot(weight.astype(BF16), tv)
        denom = jnp.broadcast_to(jnp.sum(weight, 1, keepdims=True), (32, 128))
        s.treen[4 * b:4 * b + 4] = numer.reshape(4, 8, HEAD)
        s.treed[4 * b:4 * b + 4] = denom.reshape(4, 8, 128)

    for copy in in_h:
        copy.wait()
    drain(s.precv, s.pr)
    inner = lax.fori_loop(
        0, CHIPS - 1,
        lambda i, acc: acc + s.precv[i].astype(F32),
        s.psum[chip].astype(F32),
    )
    fresh = (s.hown[...].astype(F32) + inner / (1.0 + jnp.exp(-inner))).astype(BF16)
    s.f0[my, mc, mx, mz] = fresh[0]
    s.f1[mx, mc, my, mz] = fresh[1]
    lines = ((s.f0, my, mx, x_peer, y_peer), (s.f1, mx, my, y_peer, x_peer))
    for which, (buf, slow, quick, near, far) in enumerate(lines):
        own = buf.at[slow, mc, quick, mz]
        for step in range(1, 4):
            remote(own, own, s.fz_s.at[which], s.fz_r.at[which], mp=z_of(step)).start()
    for step in range(1, 4):
        for which, (buf, slow, quick, near, far) in enumerate(lines):
            own = buf.at[slow, mc, quick, mz]
            for up in range(4):
                remote(
                    own, own, s.fa_s.at[which], s.fa_r.at[which, step - 1],
                    blk=near(step), mp=z_of(up),
                ).start()

    def to_sibling(which, block):
        remote(block, block, s.fc_s.at[which], s.fc_r.at[which], blk=sibling).start()

    def pass_on(part):
        blocks = [
            buf.at[slow, mc, lax.rem(quick - part + 4, 4)]
            for buf, slow, quick, near, far in lines
        ]
        for step in (1, 3, 2):
            for which, block in enumerate(blocks):
                remote(
                    block, block, s.fb_s.at[which], s.fb_r.at[which, step - 1, part],
                    blk=lines[which][4](step),
                ).start()
        for which, block in enumerate(blocks):
            to_sibling(which, block)

    def far_came(part):
        for step in range(1, 4):
            for which, (buf, slow, quick, near, far) in enumerate(lines):
                block = buf.at[
                    lax.rem(slow - step + 4, 4), mc, lax.rem(quick - part + 4, 4)
                ]
                drain(block, s.fb_r.at[which, step - 1, part])
                to_sibling(which, block)

    def line_came():
        for which, (buf, slow, quick, near, far) in enumerate(lines):
            drain(buf.at[slow, mc, quick, pl.ds(0, 3)], s.fz_r.at[which])
        pass_on(0)

    drain(s.arecv.at[pl.ds(1, NB - 1)], s.ar)
    for half in range(2):
        def add(i, carry):
            got = s.arecv[i].astype(F32)
            named = jnp.broadcast_to(got[7:8], (8, HEAD))
            return tuple(
                acc + jnp.where(named == float(half * 6 + g), got, 0.0)
                for g, acc in enumerate(carry)
            )

        sums = lax.fori_loop(0, NB, add, (jnp.zeros((8, HEAD), F32),) * 6)
        for g in range(6):
            spots = jnp.broadcast_to(sums[g][6:7, :128], (8, 128))
            spots = jnp.where((lane_l == row_l) | (lane_l == row_l + 8), spots, 0.0)
            denom = jnp.sum(spots, 1, keepdims=True) + s.treed[half * 6 + g][:, :1]
            denom = jnp.where(iota((8, 1), 0) < 6, denom, 1.0)
            numer = sums[g] + s.treen[half * 6 + g]
            numer = jnp.where(row8 < 6, numer, 0.0)
            s.hbuf[half * 6 + g] = (numer / denom).astype(BF16)

    def heads_copy(g):
        chunk = g * 8 + part
        owner = chunk // 3
        spot = (chunk % 3) * 4 + head
        return owner, spot

    def send_heads(g, carry):
        owner, spot = heads_copy(g)

        @pl.when(owner != me)
        def _():
            remote(
                s.hbuf.at[g], s.hrecv.at[spot], s.hs.at[g], s.hr, blk=owner
            ).start()

        @pl.when(owner == me)
        def _():
            pltpu.make_async_copy(s.hbuf.at[g], s.hrecv.at[spot], s.hr).start()

        return carry

    lax.fori_loop(0, GROUPS, send_heads, 0)

    line_came()
    for step in range(1, 4):
        for which, (buf, slow, quick, near, far) in enumerate(lines):
            came = buf.at[slow, mc, lax.rem(quick - step + 4, 4)]
            drain(came, s.fa_r.at[which, step - 1])
        pass_on(step)
    far_came(0)

    in_o.wait()
    drain(s.hrecv, s.hr)
    lhs = jnp.concatenate(
        [
            jnp.concatenate([s.hrecv[t * 4 + h].astype(F32) for h in range(HEADS)], 1)
            for t in range(3)
        ],
        0,
    ).astype(BF16)
    for tile in range(7):
        cols = slice(tile * 512, tile * 512 + 512)
        got = dot(lhs, s.outv[:, cols]).astype(BF16)
        s.zbuf[mz, :, :, cols] = got.reshape(3, 8, 512)
    for step in range(1, 4):
        own = s.zbuf.at[mz]
        remote(own, own, s.zs, s.zr, mp=z_of(step)).start()

    in_c.wait()
    s.idv[...] = jnp.zeros((2, 16, 384), F32)
    for m in range(2):
        s.idv[m, 0:TOPC, 0:ROWS] = s.candv[:, m, :].astype(F32)
    ids = s.idv[0] + pltpu.roll(s.idv[1], ROWS, 1)
    base = ((me * 4 + mz) * VOCAB).astype(F32)
    ids = jnp.concatenate([ids - base, jnp.zeros((112, 384), F32)], 0).T
    for c in range(TOPC):
        s.idb[c] = jnp.broadcast_to(ids[:MROWS, c:c + 1], (MROWS, 128))

    for late in range(1, 4):
        far_came(late)

    def arrange(core):
        def body(one, carry):
            x, y = one // 4, one % 4
            for p in range(2):
                chunk = 4 * one + 2 * core + p
                row = pl.multiple_of((chunk // 7) * 32, 32)

                @pl.when(chunk < 63)
                def _():
                    for z in range(4):
                        col = pl.multiple_of(z * UNITS + (chunk % 7) * 128, 128)
                        piece = s.f0[y, core, x, z] if p == 0 else s.f1[x, core, y, z]
                        s.fresh[pl.ds(row, 32), pl.ds(col, 128)] = piece

            return carry

        lax.fori_loop(0, CHIPS, body, 0)

    arrange(mc)
    for which, (buf, slow, quick, near, far) in enumerate(lines):
        drain(buf.at[pl.ds(0, 2)], s.fc_r.at[which])
    arrange(1 - mc)

    in_e.wait()
    lane = iota((16, 128), 1)
    spot = [lane.astype(F32) + 128.0 * k for k in range(VOCAB // 128)]

    def raw_tile(tile):
        return dot(s.fresh[...], s.embv[tile * 256:tile * 256 + 256, :], NT)

    def score(raw, tile):
        for strip in range(MROWS // 16):
            rows = slice(strip * 16, strip * 16 + 16)
            if tile == 0:
                total = jnp.zeros((16, 128), F32)
                picks = [total] * TOPC
            else:
                total = s.tally[TOPC, rows, :]
                picks = [s.tally[c, rows, :] for c in range(TOPC)]
            for k in range(2):
                logits = 30.0 * jnp.tanh(raw[rows, k * 128:k * 128 + 128] * (1.0 / 30.0))
                total = total + jnp.exp(logits)
                picks = [
                    jnp.where(s.idb[c, rows, :] == spot[2 * tile + k], logits, picks[c])
                    for c in range(TOPC)
                ]
            if tile < 3:
                s.tally[TOPC, rows, :] = total
                for c in range(TOPC):
                    s.tally[c, rows, :] = picks[c]
            else:
                found = jnp.where(lane == TOPC, jnp.sum(total, 1, keepdims=True), 0.0)
                for c in range(TOPC):
                    row_sum = jnp.sum(picks[c], 1, keepdims=True)
                    found = found + jnp.where(lane == c, row_sum, 0.0)
                s.cols[rows, :] = found

    s.cols[MROWS:, :] = jnp.zeros((384 - MROWS, 128), F32)
    raw = raw_tile(0)
    for tile in range(1, 4):
        ahead = raw_tile(tile)
        score(raw, tile - 1)
        raw = ahead
    score(raw, 3)
    stats = s.cols[...].T[:16]
    tall = iota((16, 384), 0)

    def pack(stats):
        total = stats[TOPC:TOPC + 1]
        high = total.astype(BF16).astype(F32)
        middle = (total - high).astype(BF16).astype(F32)
        low = total - high - middle
        stats = jnp.where(tall == TOPC, high, stats)
        stats = jnp.where(tall == TOPC + 1, middle, stats)
        return jnp.where(tall == TOPC + 2, low, stats).astype(BF16)

    def unpack(parts):
        stats = parts[0].astype(F32)
        for more in parts[1:]:
            stats = stats + more.astype(F32)
        total = stats[TOPC:TOPC + 1] + stats[TOPC + 1:TOPC + 2] + stats[TOPC + 2:TOPC + 3]
        return jnp.where(tall == TOPC, total, stats)

    def share(buf, spot, sems, targets):
        own = buf.at[spot]
        for where in targets:
            remote(own, own, *sems, **where).start()

    s.sbuf[mz * 2 + mc] = pack(stats)
    targets = [{"blk": sibling}]
    for step in range(1, 4):
        targets += [{"mp": z_of(step)}, {"blk": sibling, "mp": z_of(step)}]
    share(s.sbuf, mz * 2 + mc, (s.ss, s.sr), targets)

    for copy in in_g:
        copy.wait()
    drain(s.zbuf.at[pl.ds(0, 3)], s.zr)
    attn = s.zbuf[0].astype(F32)
    for z in range(1, 4):
        attn = attn + s.zbuf[z].astype(F32)
    mean = jnp.sum(attn * attn, -1, keepdims=True) * (1.0 / D)
    normed = attn * lax.rsqrt(mean + 1e-06) * s.gainv[...].reshape(1, 1, D)
    for t in range(3):
        s.nrm[6 * t:6 * t + 6, :] = normed[t, :6]
    s.layer[...] = (s.nrm[0:18, :] + s.residv[...].astype(F32)).astype(BF16)
    leave = pltpu.make_async_copy(s.layer, out_ref, s.sem_out)
    leave.start()

    drain(s.sbuf.at[pl.ds(0, 7)], s.sr)
    s.gbuf[chip] = pack(unpack([s.sbuf[i] for i in range(8)]))
    share(
        s.gbuf, chip, (s.gs, s.gr),
        [{"blk": 2 * chip_of(step) + mc} for step in range(1, CHIPS)],
    )
    drain(s.gbuf.at[pl.ds(0, CHIPS - 1)], s.gr)
    full = unpack([s.gbuf[i] for i in range(CHIPS)])
    found = full - jnp.log(full[TOPC:TOPC + 1])
    stat_ref[:, 0, :] = found[:TOPC, :ROWS]
    stat_ref[:, 1, :] = pltpu.roll(found, 384 - ROWS, 1)[:TOPC, :ROWS]

    leave.wait()

    drain(s.psib, s.pc_s)
    drain(s.precv, s.ps)
    drain(s.arecv.at[pl.ds(1, NB - 1)], s.as_)
    for which, (buf, slow, quick, near, far) in enumerate(lines):
        drain(buf.at[slow, mc, quick, pl.ds(0, 3)], s.fz_s.at[which])
        drain(buf.at[slow, mc, pl.ds(0, 3)], s.fa_s.at[which])
        drain(buf.at[pl.ds(0, 3), mc], s.fb_s.at[which])
        drain(buf.at[pl.ds(0, 2)], s.fc_s.at[which])

    def sent_heads(g, carry):
        owner, spot = heads_copy(g)

        @pl.when(owner != me)
        def _():
            drain(s.hbuf.at[g], s.hs.at[g])

        return carry

    lax.fori_loop(0, GROUPS, sent_heads, 0)
    drain(s.zbuf.at[pl.ds(0, 3)], s.zs)
    drain(s.sbuf.at[pl.ds(0, 7)], s.ss)
    drain(s.gbuf.at[pl.ds(0, CHIPS - 1)], s.gs)


def per_device(
    hidden, medusa_w, embedding, cand_ids, tree_q, tree_key_value, prompt_key_value,
    block_group, block_len, block_empty, parents, out_weight, post_gain, resid,
):
    anywhere = pl.BlockSpec(memory_space=pl.ANY)
    scalar = pl.BlockSpec(memory_space=pltpu.SMEM)
    whole = pl.BlockSpec(memory_space=pltpu.VMEM)
    layer_out, stats = pl.pallas_call(
        kernel,
        out_shape=(
            jax.ShapeDtypeStruct((18, D), BF16),
            jax.ShapeDtypeStruct((TOPC, 2, ROWS), F32),
        ),
        in_specs=[anywhere] * 7 + [scalar] * 3 + [anywhere] * 4,
        out_specs=(anywhere, whole),
        scratch_shapes=[kind for _, kind in SCRATCH],
        compiler_params=pltpu.CompilerParams(
            collective_id=0, has_side_effects=True, vmem_limit_bytes=60 << 20
        ),
    )(
        hidden, medusa_w, embedding, cand_ids.transpose(2, 0, 1), tree_q, tree_key_value,
        prompt_key_value, block_group, block_len, block_empty, parents, out_weight,
        post_gain, resid,
    )
    return (stats.transpose(1, 2, 0), layer_out)


def solution(mesh):
    placed = (
        P(),
        P(None, "blk", "mp"),
        P(("blk", "mp"), None),
        P(),
        P(None, None, "mp"),
        P(None, None, None, "mp"),
        P(None, "blk", None, "mp"),
        P("blk"),
        P("blk"),
        P("blk"),
        P(),
        P("mp", None),
        P(),
        P("blk", None),
    )
    return jax.shard_map(
        per_device, mesh=mesh, in_specs=placed, out_specs=(P(), P("blk", None)), check_vma=False
    )
```

```python
import jax
import jax.numpy as jnp
from jax import lax
from jax.experimental import pallas as pl
from jax.experimental.pallas import tpu as pltpu
from jax.sharding import PartitionSpec as P

MESH = pl.DeviceIdType.MESH
F32 = jnp.float32
BF16 = jnp.bfloat16

D = 3584
ROWS = 144
MROWS = 288
UNITS = 896
DEPTH = 112
GROUPS = 12
TREE = 48
HEAD = 256
HEADS = 4
SLOTS = 2048
VOCAB = 1024
TOPC = 10
NB = 32
CHIPS = 16
KEY_TILE = 512
NT = (((1,), (1,)), ((), ()))
NN = (((1,), (0,)), ((), ()))


def dot(a, b, dims=NN):
    return lax.dot_general(a, b, dims, preferred_element_type=F32)


def iota(shape, axis):
    return lax.broadcasted_iota(jnp.int32, shape, axis)


def weigh(scores):
    return jnp.exp(50.0 * jnp.tanh(scores * (HEAD ** (-0.5) / 50.0)))


SCRATCH = (
    ("hwin", pltpu.VMEM((ROWS, 256), BF16)),
    ("wpad", pltpu.VMEM((2, 256, UNITS), BF16)),
    ("hown", pltpu.VMEM((2, 32, 128), BF16)),
    ("embv", pltpu.VMEM((VOCAB, D), BF16)),
    ("outv", pltpu.VMEM((HEADS * HEAD, D), BF16)),
    ("kbuf", pltpu.VMEM((SLOTS, 512), BF16)),
    ("vbuf", pltpu.VMEM((SLOTS, 512), BF16)),
    ("qbuf", pltpu.VMEM((GROUPS, TREE, 1024), BF16)),
    ("tqb", pltpu.VMEM((GROUPS, 64, HEAD), BF16)),
    ("tkb", pltpu.VMEM((GROUPS, 64, HEAD), BF16)),
    ("tvb", pltpu.VMEM((GROUPS, 64, HEAD), BF16)),
    ("candv", pltpu.VMEM((TOPC, 2, ROWS), jnp.int32)),
    ("parv", pltpu.VMEM((GROUPS, TREE), jnp.int32)),
    ("gainv", pltpu.VMEM((D,), F32)),
    ("residv", pltpu.VMEM((18, D), BF16)),
    ("sem_in", pltpu.SemaphoreType.DMA((20,))),
    ("pbuf", pltpu.VMEM((2, CHIPS, 2, 32, 128), BF16)),
    ("psib", pltpu.VMEM((2, CHIPS, 32, 128), BF16)),
    ("psum", pltpu.VMEM((2, CHIPS, 32, 128), BF16)),
    ("precv", pltpu.VMEM((2, CHIPS - 1, 32, 128), BF16)),
    ("pc_s", pltpu.SemaphoreType.DMA((2,))),
    ("pc_r", pltpu.SemaphoreType.DMA((2,))),
    ("ps", pltpu.SemaphoreType.DMA((2,))),
    ("pr", pltpu.SemaphoreType.DMA((2,))),
    ("f0", pltpu.VMEM((4, 2, 4, 4, 32, 128), BF16)),
    ("f1", pltpu.VMEM((4, 2, 4, 4, 32, 128), BF16)),
    ("fz_s", pltpu.SemaphoreType.DMA((2,))),
    ("fz_r", pltpu.SemaphoreType.DMA((2,))),
    ("fa_s", pltpu.SemaphoreType.DMA((2,))),
    ("fa_r", pltpu.SemaphoreType.DMA((2, 3))),
    ("fb_s", pltpu.SemaphoreType.DMA((2,))),
    ("fb_r", pltpu.SemaphoreType.DMA((2, 3, 4))),
    ("fc_s", pltpu.SemaphoreType.DMA((2,))),
    ("fc_r", pltpu.SemaphoreType.DMA((2,))),
    ("fresh", pltpu.VMEM((MROWS, D), BF16)),
    ("abuf", pltpu.VMEM((NB, 8, HEAD), BF16)),
    ("arecv", pltpu.VMEM((NB, 8, HEAD), BF16)),
    ("as_", pltpu.SemaphoreType.DMA),
    ("ar", pltpu.SemaphoreType.DMA),
    ("treen", pltpu.VMEM((GROUPS, 8, HEAD), F32)),
    ("treed", pltpu.VMEM((GROUPS, 8, 128), F32)),
    ("hbuf", pltpu.VMEM((GROUPS, 8, HEAD), BF16)),
    ("hrecv", pltpu.VMEM((GROUPS, 8, HEAD), BF16)),
    ("hs", pltpu.SemaphoreType.DMA((GROUPS,))),
    ("hr", pltpu.SemaphoreType.DMA),
    ("zbuf", pltpu.VMEM((4, 3, 8, D), BF16)),
    ("zs", pltpu.SemaphoreType.DMA),
    ("zr", pltpu.SemaphoreType.DMA),
    ("nrm", pltpu.VMEM((24, D), F32)),
    ("layer", pltpu.VMEM((18, D), BF16)),
    ("sem_out", pltpu.SemaphoreType.DMA),
    ("idv", pltpu.VMEM((2, 16, 384), F32)),
    ("idb", pltpu.VMEM((TOPC, MROWS, 128), F32)),
    ("tally", pltpu.VMEM((TOPC + 1, MROWS, 128), F32)),
    ("cols", pltpu.VMEM((384, 128), F32)),
    ("sbuf", pltpu.VMEM((8, 16, 384), BF16)),
    ("ss", pltpu.SemaphoreType.DMA),
    ("sr", pltpu.SemaphoreType.DMA),
    ("gbuf", pltpu.VMEM((CHIPS, 16, 384), BF16)),
    ("gs", pltpu.SemaphoreType.DMA),
    ("gr", pltpu.SemaphoreType.DMA),
)


class Refs:
    pass


def kernel(
    hidden, medusa_w, embedding, cand_ids, tree_q, tree_kv, prompt_kv,
    block_group, block_len, block_empty, parents, out_weight, post_gain, resid,
    out_ref, stat_ref, *scratch
):
    s = Refs()
    for (name, _), ref in zip(SCRATCH, scratch):
        setattr(s, name, ref)
    me = lax.axis_index("blk")
    mz = lax.axis_index("mp")
    chip, mc = me // 2, me % 2
    mx, my = chip // 4, chip % 4
    sibling = me + 1 - 2 * mc
    head, part = me // 8, me % 8

    def peer_of(step):
        return lax.rem(me + step, NB)

    def chip_of(step):
        return lax.rem(chip + step, CHIPS)

    def z_of(step):
        return lax.rem(mz + step, 4)

    def x_peer(step):
        return lax.rem(mx + step, 4) * 8 + my * 2 + mc

    def y_peer(step):
        return mx * 8 + lax.rem(my + step, 4) * 2 + mc

    def remote(src, dst, ss, rs, **where):
        return pltpu.make_async_remote_copy(
            src_ref=src, dst_ref=dst, send_sem=ss, recv_sem=rs,
            device_id=where, device_id_type=MESH,
        )

    def drain(ref, sem):
        pltpu.make_async_copy(ref, ref, sem).wait()

    barrier = pltpu.get_barrier_semaphore()

    def greet(step, carry):
        pl.semaphore_signal(
            barrier, inc=1, device_id={"blk": peer_of(step)}, device_id_type=MESH
        )
        return carry

    lax.fori_loop(1, NB, greet, 0)
    for step in range(1, 4):
        pl.semaphore_signal(
            barrier, inc=1, device_id={"mp": z_of(step)}, device_id_type=MESH
        )
        pl.semaphore_signal(
            barrier, inc=1, device_id={"blk": sibling, "mp": z_of(step)}, device_id_type=MESH
        )

    for up in range(1, 4):
        for step in range(1, 4):
            for peer in (x_peer(step), y_peer(step)):
                pl.semaphore_signal(
                    barrier, inc=1, device_id={"blk": peer, "mp": z_of(up)},
                    device_id_type=MESH,
                )

    inputs = []

    def fetch(src, dst):
        copy = pltpu.make_async_copy(src, dst, s.sem_in.at[len(inputs)])
        copy.start()
        inputs.append(copy)
        return copy

    first = DEPTH * me
    start = jnp.minimum((first // 128) * 128, D - 256)
    start = pl.multiple_of(start, 128)
    shift = pl.multiple_of(first - start, 16)
    for m in range(2):
        s.wpad[m] = jnp.zeros((256, UNITS), BF16)
    in_w = [
        fetch(hidden.at[:, pl.ds(start, 256)], s.hwin),
        fetch(medusa_w.at[0], s.wpad.at[0, pl.ds(shift, DEPTH), :]),
        fetch(medusa_w.at[1], s.wpad.at[1, pl.ds(shift, DEPTH), :]),
    ]
    in_q = fetch(tree_q, s.qbuf)
    in_k = fetch(prompt_kv.at[0, 0], s.kbuf)
    in_v = fetch(prompt_kv.at[1, 0], s.vbuf)
    in_h = []
    for p in range(2):
        chunk = 2 * me + p
        rblk, lane = chunk // 7, chunk % 7
        col = pl.multiple_of(mz * UNITS + lane * 128, 128)
        for half in range(2):
            row = pl.multiple_of(((rblk * 2 + half) % 9) * 16, 16)
            in_h.append(
                fetch(
                    hidden.at[pl.ds(row, 16), pl.ds(col, 128)],
                    s.hown.at[p, pl.ds(half * 16, 16), :],
                )
            )
    qcol = pl.multiple_of(head * HEAD, HEAD)
    kcol = pl.multiple_of((head // 2) * HEAD, HEAD)
    in_t = [
        fetch(tree_q.at[:, :, pl.ds(qcol, HEAD)], s.tqb.at[:, pl.ds(0, TREE), :]),
        fetch(tree_kv.at[0, :, :, pl.ds(kcol, HEAD)], s.tkb.at[:, pl.ds(0, TREE), :]),
        fetch(tree_kv.at[1, :, :, pl.ds(kcol, HEAD)], s.tvb.at[:, pl.ds(0, TREE), :]),
        fetch(parents, s.parv),
    ]
    in_c = fetch(cand_ids, s.candv)
    in_o = fetch(out_weight, s.outv)
    in_g = [fetch(post_gain, s.gainv), fetch(resid, s.residv)]
    in_e = fetch(embedding, s.embv)

    for copy in in_w:
        copy.wait()
    hwin = s.hwin[...]
    for m in range(2):
        product = dot(hwin, s.wpad[m]).astype(BF16)
        for u in range(9):
            unit = m * 9 + u
            for lane in range(7):
                chunk = (unit // 2) * 7 + lane
                low = (unit % 2) * 16
                s.pbuf[chunk % 2, chunk // 4, chunk // 2 % 2, low:low + 16, :] = (
                    product[u * 16:u * 16 + 16, lane * 128:lane * 128 + 128]
                )
    s.pbuf[1, CHIPS - 1, 1] = jnp.zeros((32, 128), BF16)
    pl.semaphore_wait(barrier, NB - 1 + 6 + 18)
    for p in range(2):
        remote(
            s.pbuf.at[p, :, 1 - mc], s.psib.at[p], s.pc_s.at[p], s.pc_r.at[p], blk=sibling
        ).start()
    for p in range(2):
        drain(s.psib.at[p], s.pc_r.at[p])
        s.psum[p] = (s.pbuf[p, :, mc].astype(F32) + s.psib[p].astype(F32)).astype(BF16)
        for step in range(1, CHIPS):
            to = chip_of(step)
            remote(
                s.psum.at[p, to], s.precv.at[p, step - 1], s.ps.at[p], s.pr.at[p],
                blk=2 * to + mc,
            ).start()

    group = block_group[0]
    limit = jnp.where(block_empty[0] == 0, block_len[0], 0)
    spread = (
        (iota((64, TREE), 0) // 8) * 6 + iota((64, TREE), 0) % 8 == iota((64, TREE), 1)
    ) & (iota((64, TREE), 0) % 8 < 6)
    spread = spread.astype(F32).astype(BF16)
    in_q.wait()
    queries = dot(spread, s.qbuf[group]).astype(BF16)
    in_k.wait()
    in_v.wait()
    row8 = iota((8, HEAD), 0)
    row_l = iota((8, 128), 0)
    lane_l = iota((8, 128), 1)
    tag = jnp.full((8, HEAD), group, jnp.int32).astype(F32)
    for kv in range(2):
        cols = slice(kv * HEAD, kv * HEAD + HEAD)
        two = jnp.concatenate(
            [queries[:, (2 * kv + r) * HEAD:(2 * kv + r + 1) * HEAD] for r in range(2)], 0
        )
        numer = jnp.zeros((128, HEAD), F32)
        denom = jnp.zeros((128, 128), F32)
        for tile in range(SLOTS // KEY_TILE):
            keys = slice(tile * KEY_TILE, tile * KEY_TILE + KEY_TILE)
            seen = iota((128, KEY_TILE), 1) + tile * KEY_TILE < limit
            weight = jnp.where(seen, weigh(dot(two, s.kbuf[keys, cols], NT)), 0.0)
            for piece in range(KEY_TILE // 128):
                denom = denom + weight[:, piece * 128:piece * 128 + 128]
            numer = numer + dot(weight.astype(BF16), s.vbuf[keys, cols])
        total = jnp.broadcast_to(jnp.sum(denom, 1, keepdims=True), (128, 128))
        high = total.astype(BF16).astype(F32)
        rest = total - high
        for r in range(2):
            for q in range(8):
                rows = slice(r * 64 + q * 8, r * 64 + q * 8 + 8)
                spots = jnp.where(lane_l == row_l, high[rows], 0.0) + jnp.where(
                    lane_l == row_l + 8, rest[rows], 0.0
                )
                spots = jnp.sum(jnp.where(row_l < 6, spots, 0.0), 0, keepdims=True)
                spots = jnp.concatenate([spots, jnp.zeros((1, 128), F32)], 1)
                piece = jnp.where(row8 < 6, numer[rows], jnp.where(row8 == 6, spots, tag))
                s.abuf[(2 * kv + r) * 8 + q] = piece.astype(BF16)

    def send_attention(step, carry):
        peer = peer_of(step)
        remote(s.abuf.at[peer], s.arecv.at[step], s.as_, s.ar, blk=peer).start()
        return carry

    lax.fori_loop(1, NB, send_attention, 0)
    s.arecv[0] = s.abuf[me]

    for copy in in_t:
        copy.wait()
    for buf in (s.tqb, s.tkb, s.tvb):
        for g in range(GROUPS):
            buf[g, TREE:64, :] = jnp.zeros((64 - TREE, HEAD), BF16)
    place = (iota((TREE, 256), 0) == iota((TREE, 256), 1) % 64).astype(F32).astype(BF16)
    spots = dot(s.parv[...].astype(F32).astype(BF16), place)
    sub = iota((256, 256), 0)
    lan = iota((256, 256), 1)
    eye = sub == lan
    pick_row = iota((32, 256), 0)
    pick_col = iota((32, 256), 1)
    pick = (pick_col == (pick_row // 8) * 64 + part * 6 + pick_row % 8) & (pick_row % 8 < 6)
    pick = pick.astype(F32).astype(BF16)
    for b in range(3):
        mine = iota((GROUPS, 256), 0) == 4 * b + iota((GROUPS, 256), 1) // 64
        parent = jnp.sum(jnp.where(mine, spots, 0.0), 0, keepdims=True)
        wanted = parent + (iota((1, 256), 1) // 64 * 64).astype(F32)
        linked = (sub.astype(F32) == wanted) & (lan % 64 > 0)
        reach = jnp.where(eye | linked, 1.0, 0.0).astype(BF16)
        for sweep in range(6):
            reach = jnp.minimum(dot(reach, reach), 1.0).astype(BF16)
        mask = dot(pick, reach, NT)
        tq = s.tqb[4 * b:4 * b + 4].reshape(256, HEAD)
        tk = s.tkb[4 * b:4 * b + 4].reshape(256, HEAD)
        tv = s.tvb[4 * b:4 * b + 4].reshape(256, HEAD)
        rows = dot(pick, tq).astype(BF16)
        weight = weigh(dot(rows, tk, NT)) * mask
        numer = dot(weight.astype(BF16), tv)
        denom = jnp.broadcast_to(jnp.sum(weight, 1, keepdims=True), (32, 128))
        s.treen[4 * b:4 * b + 4] = numer.reshape(4, 8, HEAD)
        s.treed[4 * b:4 * b + 4] = denom.reshape(4, 8, 128)

    for copy in in_h:
        copy.wait()
    lines = ((s.f0, my, mx, x_peer, y_peer), (s.f1, mx, my, y_peer, x_peer))
    for which, (buf, slow, quick, near, far) in enumerate(lines):
        drain(s.precv.at[which], s.pr.at[which])
        inner = s.psum[which, chip].astype(F32)
        for i in range(CHIPS - 1):
            inner = inner + s.precv[which, i].astype(F32)
        fresh = s.hown[which].astype(F32) + inner / (1.0 + jnp.exp(-inner))
        buf[slow, mc, quick, mz] = fresh.astype(BF16)
        own = buf.at[slow, mc, quick, mz]
        for step in range(1, 4):
            remote(own, own, s.fz_s.at[which], s.fz_r.at[which], mp=z_of(step)).start()
        for step in range(1, 4):
            for up in range(4):
                remote(
                    own, own, s.fa_s.at[which], s.fa_r.at[which, step - 1],
                    blk=near(step), mp=z_of(up),
                ).start()

    def to_sibling(which, block):
        remote(block, block, s.fc_s.at[which], s.fc_r.at[which], blk=sibling).start()

    def pass_on(part):
        blocks = [
            buf.at[slow, mc, lax.rem(quick - part + 4, 4)]
            for buf, slow, quick, near, far in lines
        ]
        for step in (1, 3, 2):
            for which, block in enumerate(blocks):
                remote(
                    block, block, s.fb_s.at[which], s.fb_r.at[which, step - 1, part],
                    blk=lines[which][4](step),
                ).start()
        for which, block in enumerate(blocks):
            to_sibling(which, block)

    def far_came(part):
        for step in range(1, 4):
            for which, (buf, slow, quick, near, far) in enumerate(lines):
                block = buf.at[
                    lax.rem(slow - step + 4, 4), mc, lax.rem(quick - part + 4, 4)
                ]
                drain(block, s.fb_r.at[which, step - 1, part])
                to_sibling(which, block)

    def line_came():
        for which, (buf, slow, quick, near, far) in enumerate(lines):
            drain(buf.at[slow, mc, quick, pl.ds(0, 3)], s.fz_r.at[which])
        pass_on(0)

    drain(s.arecv.at[pl.ds(1, NB - 1)], s.ar)
    for half in range(2):
        def add(i, carry):
            got = s.arecv[i].astype(F32)
            named = jnp.broadcast_to(got[7:8], (8, HEAD))
            return tuple(
                acc + jnp.where(named == float(half * 6 + g), got, 0.0)
                for g, acc in enumerate(carry)
            )

        sums = lax.fori_loop(0, NB, add, (jnp.zeros((8, HEAD), F32),) * 6)
        for g in range(6):
            spots = jnp.broadcast_to(sums[g][6:7, :128], (8, 128))
            spots = jnp.where((lane_l == row_l) | (lane_l == row_l + 8), spots, 0.0)
            denom = jnp.sum(spots, 1, keepdims=True) + s.treed[half * 6 + g][:, :1]
            denom = jnp.where(iota((8, 1), 0) < 6, denom, 1.0)
            numer = sums[g] + s.treen[half * 6 + g]
            numer = jnp.where(row8 < 6, numer, 0.0)
            s.hbuf[half * 6 + g] = (numer / denom).astype(BF16)

    def heads_copy(g):
        chunk = g * 8 + part
        owner = chunk // 3
        spot = (chunk % 3) * 4 + head
        return owner, spot

    def send_heads(g, carry):
        owner, spot = heads_copy(g)

        @pl.when(owner != me)
        def _():
            remote(
                s.hbuf.at[g], s.hrecv.at[spot], s.hs.at[g], s.hr, blk=owner
            ).start()

        @pl.when(owner == me)
        def _():
            pltpu.make_async_copy(s.hbuf.at[g], s.hrecv.at[spot], s.hr).start()

        return carry

    lax.fori_loop(0, GROUPS, send_heads, 0)

    line_came()
    for step in range(1, 4):
        for which, (buf, slow, quick, near, far) in enumerate(lines):
            came = buf.at[slow, mc, lax.rem(quick - step + 4, 4)]
            drain(came, s.fa_r.at[which, step - 1])
        pass_on(step)
    far_came(0)

    in_o.wait()
    drain(s.hrecv, s.hr)
    lhs = jnp.concatenate(
        [
            jnp.concatenate([s.hrecv[t * 4 + h].astype(F32) for h in range(HEADS)], 1)
            for t in range(3)
        ],
        0,
    ).astype(BF16)
    for tile in range(7):
        cols = slice(tile * 512, tile * 512 + 512)
        got = dot(lhs, s.outv[:, cols]).astype(BF16)
        s.zbuf[mz, :, :, cols] = got.reshape(3, 8, 512)
    for step in range(1, 4):
        own = s.zbuf.at[mz]
        remote(own, own, s.zs, s.zr, mp=z_of(step)).start()

    in_c.wait()
    s.idv[...] = jnp.zeros((2, 16, 384), F32)
    for m in range(2):
        s.idv[m, 0:TOPC, 0:ROWS] = s.candv[:, m, :].astype(F32)
    ids = s.idv[0] + pltpu.roll(s.idv[1], ROWS, 1)
    base = ((me * 4 + mz) * VOCAB).astype(F32)
    ids = jnp.concatenate([ids - base, jnp.zeros((112, 384), F32)], 0).T
    for c in range(TOPC):
        s.idb[c] = jnp.broadcast_to(ids[:MROWS, c:c + 1], (MROWS, 128))

    for late in range(1, 4):
        far_came(late)

    def arrange(core, lots):
        def body(one, carry):
            x, y = one // 4, one % 4
            for p in lots:
                chunk = 4 * one + 2 * core + p
                row = pl.multiple_of((chunk // 7) * 32, 32)

                @pl.when(chunk < 63)
                def _():
                    for z in range(4):
                        col = pl.multiple_of(z * UNITS + (chunk % 7) * 128, 128)
                        piece = s.f0[y, core, x, z] if p == 0 else s.f1[x, core, y, z]
                        s.fresh[pl.ds(row, 32), pl.ds(col, 128)] = piece

            return carry

        lax.fori_loop(0, CHIPS, body, 0)

    arrange(mc, (0, 1))
    for which, (buf, slow, quick, near, far) in enumerate(lines):
        drain(buf.at[pl.ds(0, 2)], s.fc_r.at[which])
        arrange(1 - mc, (which,))

    in_e.wait()
    lane = iota((16, 128), 1)
    spot = [lane.astype(F32) + 128.0 * k for k in range(VOCAB // 128)]

    def raw_tile(tile):
        return dot(s.fresh[...], s.embv[tile * 256:tile * 256 + 256, :], NT)

    def score(raw, tile):
        for strip in range(MROWS // 16):
            rows = slice(strip * 16, strip * 16 + 16)
            if tile == 0:
                total = jnp.zeros((16, 128), F32)
                picks = [total] * TOPC
            else:
                total = s.tally[TOPC, rows, :]
                picks = [s.tally[c, rows, :] for c in range(TOPC)]
            for k in range(2):
                logits = 30.0 * jnp.tanh(raw[rows, k * 128:k * 128 + 128] * (1.0 / 30.0))
                total = total + jnp.exp(logits)
                picks = [
                    jnp.where(s.idb[c, rows, :] == spot[2 * tile + k], logits, picks[c])
                    for c in range(TOPC)
                ]
            if tile < 3:
                s.tally[TOPC, rows, :] = total
                for c in range(TOPC):
                    s.tally[c, rows, :] = picks[c]
            else:
                found = jnp.where(lane == TOPC, jnp.sum(total, 1, keepdims=True), 0.0)
                for c in range(TOPC):
                    row_sum = jnp.sum(picks[c], 1, keepdims=True)
                    found = found + jnp.where(lane == c, row_sum, 0.0)
                s.cols[rows, :] = found

    s.cols[MROWS:, :] = jnp.zeros((384 - MROWS, 128), F32)
    raw = raw_tile(0)
    for tile in range(1, 4):
        ahead = raw_tile(tile)
        score(raw, tile - 1)
        raw = ahead
    score(raw, 3)
    stats = s.cols[...].T[:16]
    tall = iota((16, 384), 0)

    def pack(stats):
        total = stats[TOPC:TOPC + 1]
        high = total.astype(BF16).astype(F32)
        middle = (total - high).astype(BF16).astype(F32)
        low = total - high - middle
        stats = jnp.where(tall == TOPC, high, stats)
        stats = jnp.where(tall == TOPC + 1, middle, stats)
        return jnp.where(tall == TOPC + 2, low, stats).astype(BF16)

    def unpack(parts):
        stats = parts[0].astype(F32)
        for more in parts[1:]:
            stats = stats + more.astype(F32)
        total = stats[TOPC:TOPC + 1] + stats[TOPC + 1:TOPC + 2] + stats[TOPC + 2:TOPC + 3]
        return jnp.where(tall == TOPC, total, stats)

    def share(buf, spot, sems, targets):
        own = buf.at[spot]
        for where in targets:
            remote(own, own, *sems, **where).start()

    s.sbuf[mz * 2 + mc] = pack(stats)
    targets = [{"blk": sibling}]
    for step in range(1, 4):
        targets += [{"mp": z_of(step)}, {"blk": sibling, "mp": z_of(step)}]
    share(s.sbuf, mz * 2 + mc, (s.ss, s.sr), targets)

    for copy in in_g:
        copy.wait()
    drain(s.zbuf.at[pl.ds(0, 3)], s.zr)
    attn = s.zbuf[0].astype(F32)
    for z in range(1, 4):
        attn = attn + s.zbuf[z].astype(F32)
    mean = jnp.sum(attn * attn, -1, keepdims=True) * (1.0 / D)
    normed = attn * lax.rsqrt(mean + 1e-06) * s.gainv[...].reshape(1, 1, D)
    for t in range(3):
        s.nrm[6 * t:6 * t + 6, :] = normed[t, :6]
    s.layer[...] = (s.nrm[0:18, :] + s.residv[...].astype(F32)).astype(BF16)
    leave = pltpu.make_async_copy(s.layer, out_ref, s.sem_out)
    leave.start()

    drain(s.sbuf.at[pl.ds(0, 7)], s.sr)
    s.gbuf[chip] = pack(unpack([s.sbuf[i] for i in range(8)]))
    share(
        s.gbuf, chip, (s.gs, s.gr),
        [{"blk": 2 * chip_of(step) + mc} for step in range(1, CHIPS)],
    )
    drain(s.gbuf.at[pl.ds(0, CHIPS - 1)], s.gr)
    full = unpack([s.gbuf[i] for i in range(CHIPS)])
    found = full - jnp.log(full[TOPC:TOPC + 1])
    stat_ref[:, 0, :] = found[:TOPC, :ROWS]
    stat_ref[:, 1, :] = pltpu.roll(found, 384 - ROWS, 1)[:TOPC, :ROWS]

    leave.wait()

    for p in range(2):
        drain(s.psib.at[p], s.pc_s.at[p])
        drain(s.precv.at[p], s.ps.at[p])
    drain(s.arecv.at[pl.ds(1, NB - 1)], s.as_)
    for which, (buf, slow, quick, near, far) in enumerate(lines):
        drain(buf.at[slow, mc, quick, pl.ds(0, 3)], s.fz_s.at[which])
        drain(buf.at[slow, mc, pl.ds(0, 3)], s.fa_s.at[which])
        drain(buf.at[pl.ds(0, 3), mc], s.fb_s.at[which])
        drain(buf.at[pl.ds(0, 2)], s.fc_s.at[which])

    def sent_heads(g, carry):
        owner, spot = heads_copy(g)

        @pl.when(owner != me)
        def _():
            drain(s.hbuf.at[g], s.hs.at[g])

        return carry

    lax.fori_loop(0, GROUPS, sent_heads, 0)
    drain(s.zbuf.at[pl.ds(0, 3)], s.zs)
    drain(s.sbuf.at[pl.ds(0, 7)], s.ss)
    drain(s.gbuf.at[pl.ds(0, CHIPS - 1)], s.gs)


def per_device(
    hidden, medusa_w, embedding, cand_ids, tree_q, tree_key_value, prompt_key_value,
    block_group, block_len, block_empty, parents, out_weight, post_gain, resid,
):
    anywhere = pl.BlockSpec(memory_space=pl.ANY)
    stay = lambda array: pltpu.with_memory_space_constraint(array, pltpu.HBM)
    hidden, medusa_w, embedding, cand_ids, tree_q, tree_key_value, prompt_key_value = map(
        stay, (hidden, medusa_w, embedding, cand_ids.transpose(2, 0, 1), tree_q,
               tree_key_value, prompt_key_value)
    )
    parents, out_weight, post_gain, resid = map(
        stay, (parents, out_weight, post_gain, resid)
    )
    scalar = pl.BlockSpec(memory_space=pltpu.SMEM)
    whole = pl.BlockSpec(memory_space=pltpu.VMEM)
    layer_out, stats = pl.pallas_call(
        kernel,
        out_shape=(
            jax.ShapeDtypeStruct((18, D), BF16),
            jax.ShapeDtypeStruct((TOPC, 2, ROWS), F32),
        ),
        in_specs=[anywhere] * 7 + [scalar] * 3 + [anywhere] * 4,
        out_specs=(anywhere, whole),
        scratch_shapes=[kind for _, kind in SCRATCH],
        compiler_params=pltpu.CompilerParams(
            collective_id=0, has_side_effects=True, vmem_limit_bytes=44 << 20
        ),
    )(
        hidden, medusa_w, embedding, cand_ids, tree_q, tree_key_value,
        prompt_key_value, block_group, block_len, block_empty, parents, out_weight,
        post_gain, resid,
    )
    return (stats.transpose(1, 2, 0), layer_out)


def solution(mesh):
    placed = (
        P(),
        P(None, "blk", "mp"),
        P(("blk", "mp"), None),
        P(),
        P(None, None, "mp"),
        P(None, None, None, "mp"),
        P(None, "blk", None, "mp"),
        P("blk"),
        P("blk"),
        P("blk"),
        P(),
        P("mp", None),
        P(),
        P("blk", None),
    )
    return jax.shard_map(
        per_device, mesh=mesh, in_specs=placed, out_specs=(P(), P("blk", None)), check_vma=False
    )
```
